32 devices in a mesh: dp: 4 (over z), ctx: 8 (over y, x, core).
Axes of the slice: x: 2, y: 2, z: 4, core: 2. Of those that a mesh axis runs over, the one named last changes fastest.
Arguments:
- queries: bfloat16 [4, 1024, 2048], P('dp', 'ctx'), may hold values from -6 to 6
- keys: bfloat16 [4, 1024, 2048], P('dp', 'ctx'), may hold values from -6 to 6
- values: bfloat16 [4, 1024, 2048], P('dp', 'ctx'), may hold values from -6 to 6
- prior_state: float32 [4, 16, 128, 128], P('dp'), may hold values from -96 to 96
- norm_gain: float32 [2048], replicated, may hold values from 0.1 to 1.9
- router_weight: bfloat16 [2048, 32], replicated, may hold values from -0.125 to 0.125
- expert_ids: int32 [4, 1024, 4], P('dp', 'ctx'), may hold values from 0 to 31, all different within a row; in each aligned block of 128 rows (0 to 127, 128 to 255, ..., all dimensions but the last counted through in order) at most 24 rows name the same one
- w_gate: bfloat16 [32, 2048, 768], P(('dp', 'ctx')), may hold values from -0.125 to 0.125
- w_up: bfloat16 [32, 2048, 768], P(('dp', 'ctx')), may hold values from -0.125 to 0.125
- w_down: bfloat16 [32, 768, 2048], P(('dp', 'ctx')), may hold values from -0.21875 to 0.21875
- cotangent: bfloat16 [4, 1024, 2048], P('dp', 'ctx'), may hold values from -6 to 6
Outputs:
- output: bfloat16 [4, 1024, 2048], P('dp', 'ctx')
- grad_queries: bfloat16 [4, 1024, 2048], P('dp', 'ctx')
- grad_keys: bfloat16 [4, 1024, 2048], P('dp', 'ctx')
- grad_values: bfloat16 [4, 1024, 2048], P('dp', 'ctx')
- grad_gate: bfloat16 [32, 2048, 768], P(('dp', 'ctx'))
- grad_up: bfloat16 [32, 2048, 768], P(('dp', 'ctx'))
- grad_down: bfloat16 [32, 768, 2048], P(('dp', 'ctx'))
- grad_router: float32 [2048, 32], replicated
The draws below stay inside these ranges and needn't reach their ends.
Inputs may be any that keep to these rules, and one draw needn't show every extreme that they name: `expert_ids`: within the rows of one device (aligned blocks of 128 tokens) no expert is named more than 24 times, and in every draw some expert is named exactly 24 times there; the 4 ids of one token differ.
All inputs are finite; a program needn't handle non-finite values.
Results may differ from the reference program's by a relative error of at most 0.012.
Values may be sent and summed in bfloat16 or wider, within the bound.
No kernel may reach another device: no remote copies, remote signals or barrier semaphores. Data moves between devices by JAX's collectives and lax.ppermute only.
A program may use at most 192 MiB of HBM per device.

```python
import math
import jax
import jax.numpy as jnp
import numpy as np
from jax import lax

H = 16
DH = 128
D = 2048
FFE = 768
TOPK = 4
TOK_DEV = 128
EXPERTS = 32
CAP = 24
SEQS = 4
LENGTH = 1024
N_CTX = 8
DEVICES = 32


def level_of(own_key, extent, split, smallest, high):
    level, own = 1.0, jax.random.fold_in(own_key, 6)
    for axis_at, parts in split:
        draws = jnp.exp(jax.random.uniform(jax.random.fold_in(own, axis_at), (parts,), jnp.float32, smallest / len(split), high / len(split)))
        level = level * jnp.repeat(draws, extent[axis_at] // parts).reshape([-1 if axis == axis_at else 1 for axis in range(len(extent))])
    return level


def deal_out(stream_key, own, number, rows, count, top, most, lean):
    sequence = jax.random.permutation(stream_key, count)
    crowded, usual = load_shares(count, rows * top, most, lean, True), load_shares(count, rows * top, most, lean, False)
    places = jnp.arange(count)

    def named(sizes, offset_by):
        used = int((sizes > 0).sum())
        fixed = max(1, used // 4)
        shifted = fixed + (places - fixed + offset_by * (used - fixed)) % max(1, count - fixed)
        return jnp.zeros((count,), jnp.int32).at[sequence[jnp.where(places < fixed, places, shifted)]].set(jnp.asarray(sizes, jnp.int32))

    sizes = jnp.where(number % 4 == 0, named(crowded, number // 4), named(usual, number - number // 4 - 1))
    mixed = jax.random.permutation(jax.random.fold_in(own, 3), count)
    donor, sink = mixed[0:count // 2 * 2:2], mixed[1:count // 2 * 2:2]
    slack = jnp.minimum(sizes[donor] - 1, most - sizes[sink]) // 2
    slack = jnp.where((donor == sequence[0]) | (sink == sequence[0]) | (sizes[sink] == 0), 0, jnp.maximum(slack, 0))
    shifted = jax.random.randint(jax.random.fold_in(own, 4), (count // 2,), 0, 1 << 20) % (slack + 1)
    sizes = sizes.at[donor].add(-shifted).at[sink].add(shifted)
    items = jnp.searchsorted(jnp.cumsum(sizes), jnp.arange(rows * top), side="right").astype(jnp.int32)
    table = items.reshape(top, rows).T
    table = table[jax.random.permutation(jax.random.fold_in(own, 1), rows)]
    offset_by = jax.random.randint(jax.random.fold_in(own, 2), (rows, 1), 0, top)
    return jnp.take_along_axis(table, (jnp.arange(top)[None, :] + offset_by) % top, axis=1)


def load_shares(number_of, total, bound, skew, full):
    portions = [(1 << 20) // math.isqrt(rank ** skew) + 1 for rank in range(1, number_of + 1)]
    largest = bound if full else min(bound, max(-(-total // number_of), total * portions[0] // sum(portions)))
    least = 1 if total - largest >= number_of - 1 else 0
    holding, spare = [largest] + [least] * (number_of - 1), total - largest - least * (number_of - 1)
    while spare > 0:
        movable = [i for i in range(1, number_of) if holding[i] < largest] or [i for i in range(1, number_of) if holding[i] < bound]
        whole, remaining = sum([portions[i] for i in movable]), spare
        for i in movable:
            more = min(bound - holding[i], max(1, remaining * portions[i] // whole), spare)
            holding[i] = holding[i] + more
            spare = spare - more
    return np.array(holding)


def gaussian(rng, dims, scale, reach, shards=(), kind=jnp.bfloat16):
    gain = level_of(rng, dims, shards, -0.22, 0.18) if shards else 1.0
    array = jax.random.normal(rng, dims, jnp.float32) * scale * gain
    return jnp.minimum(jnp.maximum(array, -reach), reach).astype(kind)


def setup_inputs(seed: int = 0) -> dict:
    arg_keys = jax.random.split(jax.random.key(seed), 12)
    queries = gaussian(arg_keys[0], (SEQS, LENGTH, D), 1.0, 6.0, ((0, 4), (1, 8)))
    keys = gaussian(arg_keys[1], (SEQS, LENGTH, D), 1.0, 6.0, ((0, 4), (1, 8)))
    values = gaussian(arg_keys[2], (SEQS, LENGTH, D), 1.0, 6.0, ((0, 4), (1, 8)))
    prior_state = gaussian(arg_keys[3], (SEQS, H, DH, DH), 16.0, 96.0, ((0, 4),), jnp.float32)
    norm_gain = jnp.clip(1.0 + 0.18 * jax.random.normal(arg_keys[4], (D,), jnp.float32), 0.1, 1.9)
    router_weight = gaussian(arg_keys[5], (D, EXPERTS), D ** -0.5, 0.125)
    expert_ids_keys = jax.random.split(jax.random.fold_in(arg_keys[6], 1), SEQS * LENGTH // TOK_DEV)
    expert_ids_turns = jax.random.permutation(jax.random.fold_in(arg_keys[6], 3), SEQS * LENGTH // TOK_DEV)
    expert_ids = jax.vmap(lambda own, number: deal_out(jax.random.fold_in(arg_keys[6], 2), own, number, TOK_DEV, EXPERTS, TOPK, CAP, 2))(expert_ids_keys, expert_ids_turns).reshape((SEQS, LENGTH, TOPK))
    w_gate = gaussian(arg_keys[7], (EXPERTS, D, FFE), D ** -0.5, 0.125, ((0, 32),))
    w_up = gaussian(arg_keys[8], (EXPERTS, D, FFE), D ** -0.5, 0.125, ((0, 32),))
    w_down = gaussian(arg_keys[9], (EXPERTS, FFE, D), FFE ** -0.5, 0.21875, ((0, 32),))
    cotangent = gaussian(arg_keys[10], (SEQS, LENGTH, D), 1.0, 6.0, ((0, 4), (1, 8)))
    return dict(queries=queries, keys=keys, values=values, prior_state=prior_state, norm_gain=norm_gain, router_weight=router_weight, expert_ids=expert_ids, w_gate=w_gate, w_up=w_up, w_down=w_down, cotangent=cotangent)


epsilon = 1e-05
exact_mode = lax.Precision.HIGHEST

def expert_forward(inputs, gate_mat, up_mat, down_mat):
    gate_pre = jnp.dot(inputs, gate_mat, preferred_element_type=jnp.float32)
    up_pre = jnp.dot(inputs, up_mat, preferred_element_type=jnp.float32)
    gate_sig = jax.nn.sigmoid(gate_pre)
    hidden = (gate_pre * gate_sig * up_pre).astype(jnp.bfloat16)
    produced = jnp.dot(hidden, down_mat, preferred_element_type=jnp.float32).astype(jnp.bfloat16)
    return (gate_pre, up_pre, gate_sig, hidden, produced)

def expert_backward(inputs, grad_out, gate_pre, up_pre, gate_sig, hidden, gate_mat, up_mat, down_mat):
    grad_hidden = jnp.dot(grad_out, down_mat.T, preferred_element_type=jnp.float32)
    grad_gate_pre = (grad_hidden * up_pre * gate_sig * (1.0 + gate_pre * (1.0 - gate_sig))).astype(jnp.bfloat16)
    grad_up_pre = (grad_hidden * gate_pre * gate_sig).astype(jnp.bfloat16)
    grad_down = jnp.dot(hidden.T, grad_out, preferred_element_type=jnp.float32).astype(jnp.bfloat16)
    grad_gate = jnp.dot(inputs.T, grad_gate_pre, preferred_element_type=jnp.float32).astype(jnp.bfloat16)
    grad_up = jnp.dot(inputs.T, grad_up_pre, preferred_element_type=jnp.float32).astype(jnp.bfloat16)
    grad_inputs = (jnp.dot(grad_gate_pre, gate_mat.T, preferred_element_type=jnp.float32) + jnp.dot(grad_up_pre, up_mat.T, preferred_element_type=jnp.float32)).astype(jnp.bfloat16)
    return (grad_inputs, grad_gate, grad_up, grad_down)

def slot_layout(flat_ids):
    count_assign = flat_ids.shape[0]
    onehot = (flat_ids[:, None] == jnp.arange(EXPERTS, dtype=jnp.int32)[None, :]).astype(jnp.int32)
    before = jnp.cumsum(onehot, axis=0) - onehot
    slot_rank = lax.optimization_barrier(jnp.sum(before * onehot, axis=1))
    slot_index = (flat_ids * CAP + slot_rank).astype(jnp.int32)
    source = jnp.full((EXPERTS * CAP,), -1, jnp.int32).at[slot_index].set(jnp.arange(count_assign, dtype=jnp.int32))
    return (slot_index, source)

def pick_rows(table, index):
    return table[index]

def to_experts(token_side):
    shaped = token_side.reshape(DEVICES, EXPERTS, CAP, D)
    return jnp.transpose(shaped, (1, 0, 2, 3)).reshape(EXPERTS, DEVICES * CAP, D)

def to_tokens(expert_side):
    shaped = expert_side.reshape(EXPERTS, DEVICES, CAP, D)
    return jnp.transpose(shaped, (1, 0, 2, 3)).reshape(DEVICES, EXPERTS * CAP, D)

def reference(queries, keys, values, prior_state, norm_gain, router_weight, expert_ids, w_gate, w_up, w_down, cotangent):
    block_shape = (SEQS, N_CTX, TOK_DEV, H, DH)
    queries5 = queries.reshape(block_shape).astype(jnp.float32)
    keys5 = keys.reshape(block_shape).astype(jnp.float32)
    values5 = values.reshape(block_shape).astype(jnp.float32)
    state_terms = jnp.einsum('bcshi,bcshj->bchij', keys5, values5, precision=exact_mode)
    prefix = jnp.cumsum(state_terms, axis=1)
    earlier = jnp.concatenate([jnp.zeros_like(state_terms[:, :1]), prefix[:, :-1]], axis=1)
    state_in = prior_state[:, None] + earlier
    causal = jnp.arange(TOK_DEV)[:, None] >= jnp.arange(TOK_DEV)[None, :]
    scores = jnp.einsum('bcthd,bcshd->bchts', queries5, keys5, precision=exact_mode)
    attn_scores = jnp.where(causal, scores, 0.0).astype(jnp.bfloat16)
    intra = jnp.einsum('bchts,bcshj->bcthj', attn_scores.astype(jnp.float32), values5, precision=exact_mode)
    inter = jnp.einsum('bcthi,bchij->bcthj', queries5, state_in, precision=exact_mode)
    attended = intra + inter
    gain_heads = norm_gain.reshape(H, DH)
    mean_square = lax.optimization_barrier(jnp.mean(attended * attended, axis=-1, keepdims=True))
    scale_root = jnp.sqrt(mean_square + epsilon)
    mixed = (attended / scale_root * gain_heads).astype(jnp.bfloat16)
    mixed_rows = mixed.reshape(DEVICES, TOK_DEV, D)
    logits = jnp.einsum('ntd,de->nte', mixed_rows.astype(jnp.float32), router_weight.astype(jnp.float32), precision=exact_mode)
    ids_dev = expert_ids.reshape(DEVICES, TOK_DEV, TOPK)
    selected = jnp.take_along_axis(logits, ids_dev, axis=2)
    gate_sig_r = jax.nn.sigmoid(selected)
    sig_total = lax.optimization_barrier(jnp.sum(gate_sig_r, axis=2, keepdims=True))
    gates = gate_sig_r / sig_total
    slot_index, source = jax.vmap(slot_layout)(ids_dev.reshape(DEVICES, TOK_DEV * TOPK))
    filled = source >= 0
    row_of = jnp.where(filled, source // TOPK, 0).astype(jnp.int32)
    send_rows = jnp.where(filled[:, :, None], jax.vmap(pick_rows)(mixed_rows, row_of), jnp.zeros((), jnp.bfloat16))
    expert_in = to_experts(send_rows)

    def forward_one(packed):
        return expert_forward(packed[0], packed[1], packed[2], packed[3])[4]
    produced = lax.map(forward_one, (expert_in, w_gate, w_up, w_down))
    out_assign = jax.vmap(pick_rows)(to_tokens(produced), slot_index).reshape(DEVICES, TOK_DEV, TOPK, D)
    out_float = out_assign.astype(jnp.float32)
    moe_sum = jnp.einsum('ntk,ntkd->ntd', gates, out_float, precision=exact_mode)
    output = (mixed_rows.astype(jnp.float32) + moe_sum).astype(jnp.bfloat16)
    grad_y = cotangent.reshape(DEVICES, TOK_DEV, D).astype(jnp.float32)
    grad_gates = lax.optimization_barrier(jnp.sum(out_float * grad_y[:, :, None, :], axis=-1))
    grad_out_assign = (gates[..., None] * grad_y[:, :, None, :]).astype(jnp.bfloat16).reshape(DEVICES, TOK_DEV * TOPK, D)
    grad_rows = jnp.where(filled[:, :, None], jax.vmap(pick_rows)(grad_out_assign, jnp.where(filled, source, 0)), jnp.zeros((), jnp.bfloat16))
    grad_in = to_experts(grad_rows)

    def backward_one(packed):
        inputs, grad_out, gate_mat, up_mat, down_mat = packed
        gate_pre, up_pre, gate_sig, hidden, produced_unused = expert_forward(inputs, gate_mat, up_mat, down_mat)
        return expert_backward(inputs, grad_out, gate_pre, up_pre, gate_sig, hidden, gate_mat, up_mat, down_mat)
    grad_inputs, grad_gate, grad_up, grad_down = lax.map(backward_one, (expert_in, grad_in, w_gate, w_up, w_down))
    grad_assign = jax.vmap(pick_rows)(to_tokens(grad_inputs), slot_index).reshape(DEVICES, TOK_DEV, TOPK, D).astype(jnp.float32)
    grad_moe = jnp.einsum('ntk,ntkd->ntd', gates, grad_assign, precision=exact_mode)
    weighted_sum = lax.optimization_barrier(jnp.sum(gates * grad_gates, axis=2, keepdims=True))
    grad_selected = gate_sig_r * (1.0 - gate_sig_r) * (grad_gates - weighted_sum) / sig_total
    onehot_sel = (ids_dev[..., None] == jnp.arange(EXPERTS, dtype=jnp.int32)).astype(jnp.float32)
    grad_logits = lax.optimization_barrier(jnp.sum(grad_selected[..., None] * onehot_sel, axis=2))
    grad_router = jnp.dot(mixed_rows.reshape(DEVICES * TOK_DEV, D).astype(jnp.float32).T, grad_logits.reshape(DEVICES * TOK_DEV, EXPERTS), precision=exact_mode)
    router_back = jnp.einsum('nte,de->ntd', grad_logits, router_weight.astype(jnp.float32), precision=exact_mode)
    grad_mixed = grad_y + grad_moe + router_back
    weighted = gain_heads * grad_mixed.reshape(block_shape)
    inner = lax.optimization_barrier(jnp.sum(weighted * attended, axis=-1, keepdims=True))
    grad_attended = ((weighted - attended * (inner / (DH * (mean_square + epsilon)))) / scale_root).astype(jnp.bfloat16)
    grad_att32 = grad_attended.astype(jnp.float32)
    grad_terms = jnp.einsum('bcthi,bcthj->bchij', queries5, grad_att32, precision=exact_mode)
    suffix = jnp.flip(jnp.cumsum(jnp.flip(grad_terms, axis=1), axis=1), axis=1)
    later = jnp.concatenate([suffix[:, 1:], jnp.zeros_like(grad_terms[:, :1])], axis=1)
    grad_scores = jnp.where(causal, jnp.einsum('bcthj,bcshj->bchts', grad_att32, values5, precision=exact_mode), 0.0).astype(jnp.bfloat16)
    grad_sc32 = grad_scores.astype(jnp.float32)
    attn32 = attn_scores.astype(jnp.float32)
    grad_q = jnp.einsum('bchts,bcshi->bcthi', grad_sc32, keys5, precision=exact_mode) + jnp.einsum('bcthj,bchij->bcthi', grad_att32, state_in, precision=exact_mode)
    grad_k = jnp.einsum('bchts,bcthi->bcshi', grad_sc32, queries5, precision=exact_mode) + jnp.einsum('bcshj,bchij->bcshi', values5, later, precision=exact_mode)
    grad_v = jnp.einsum('bchts,bcthj->bcshj', attn32, grad_att32, precision=exact_mode) + jnp.einsum('bcshi,bchij->bcshj', keys5, later, precision=exact_mode)
    full_shape = (SEQS, LENGTH, D)
    return (output.reshape(full_shape), grad_q.astype(jnp.bfloat16).reshape(full_shape), grad_k.astype(jnp.bfloat16).reshape(full_shape), grad_v.astype(jnp.bfloat16).reshape(full_shape), grad_gate, grad_up, grad_down, grad_router)
```

```python
import functools

import jax
import jax.numpy as jnp
from jax import lax
from jax.experimental import pallas as pl
from jax.experimental.pallas import tpu as pltpu
from jax.sharding import PartitionSpec as P

H = 16
DH = 128
D = 2048
TOPK = 4
HB = 4
WIDTH = HB * DH
EPS = 1e-05
ALL = ("dp", "ctx")
F32 = jnp.float32
BF16 = jnp.bfloat16
LIMIT = 48 << 20


def mm(a, b):
    return jnp.dot(a, b, preferred_element_type=F32)


def mm_tn(a, b):
    return lax.dot_general(a, b, (((0,), (0,)), ((), ())), preferred_element_type=F32)


def mm_nt(a, b):
    return lax.dot_general(a, b, (((1,), (1,)), ((), ())), preferred_element_type=F32)


def halves(x):
    high = x.astype(BF16)
    return high, (x - high.astype(F32)).astype(BF16)


def thirds(x):
    high, rest = x.astype(BF16), None
    rest = x - high.astype(F32)
    middle = rest.astype(BF16)
    return high, middle, (rest - middle.astype(F32)).astype(BF16)


def causal_mask(n):
    return lax.broadcasted_iota(jnp.int32, (n, n), 0) >= lax.broadcasted_iota(jnp.int32, (n, n), 1)


def head(h):
    return slice(h * DH, (h + 1) * DH)


def call(kernel, out_shape, grid, in_specs, out_specs, scratch=(), flops=0, moved=0):
    return pl.pallas_call(
        kernel,
        out_shape=out_shape,
        grid=grid,
        in_specs=in_specs,
        out_specs=out_specs,
        scratch_shapes=scratch,
        compiler_params=pltpu.CompilerParams(vmem_limit_bytes=LIMIT),
        cost_estimate=pl.CostEstimate(flops=flops, bytes_accessed=moved, transcendentals=0),
    )


def whole(shape):
    return pl.BlockSpec(shape, lambda *_: (0,) * len(shape))


def columns(rows, width=WIDTH):
    return pl.BlockSpec((rows, width), lambda i: (0, i))


def per_head(n=HB):
    return pl.BlockSpec((n, DH, DH), lambda i: (i, 0, 0))


def route_kernel(cap, ids_ref, dy_ref, pick_ref, chosen_ref, mask_ref, send_ref):
    tokens, top = ids_ref.shape
    experts = chosen_ref.shape[1]
    rows = pick_ref.shape[0]
    lane = lax.broadcasted_iota(jnp.int32, (tokens, experts), 1)
    chosen = jnp.zeros((tokens, experts), F32)
    for j in range(top):
        chosen += (ids_ref[:, j : j + 1] == lane).astype(F32)
    count = mm(causal_mask(tokens).astype(F32).astype(BF16), chosen.astype(BF16))
    place = (chosen * count).astype(BF16)
    row = lax.broadcasted_iota(jnp.int32, (rows, experts), 0)
    first = lax.broadcasted_iota(jnp.int32, (rows, experts), 1) * cap
    owns = (row >= first) & (row < first + cap)
    wanted = jnp.sum(jnp.where(owns, row - first + 1, 0), axis=1, keepdims=True).astype(F32)
    found = mm_nt(owns.astype(F32).astype(BF16), place)
    pick = (found == wanted).astype(F32).astype(BF16)
    pick_ref[...] = pick
    chosen_ref[...] = chosen
    mask_ref[...] = mm(pick, chosen.astype(BF16)).astype(BF16)
    for c in range(D // WIDTH):
        at = slice(c * WIDTH, (c + 1) * WIDTH)
        send_ref[:, at] = mm(pick, dy_ref[:, at]).astype(BF16)


def route(ids, dy, experts, cap):
    tokens, rows = ids.shape[0], experts * cap
    return call(
        functools.partial(route_kernel, cap),
        (
            jax.ShapeDtypeStruct((rows, tokens), BF16),
            jax.ShapeDtypeStruct((tokens, experts), F32),
            jax.ShapeDtypeStruct((rows, experts), BF16),
            jax.ShapeDtypeStruct((rows, D), BF16),
        ),
        (1,),
        [whole(ids.shape), whole(dy.shape)],
        (
            whole((rows, tokens)),
            whole((tokens, experts)),
            whole((rows, experts)),
            whole((rows, D)),
        ),
        flops=2 * rows * tokens * D,
        moved=2 * rows * D,
    )(ids, dy)


def state_kernel(k_ref, v_ref, out_ref):
    for h in range(HB):
        out_ref[h] = mm_tn(k_ref[:, head(h)], v_ref[:, head(h)]).astype(BF16)


def state_terms(k, v):
    tokens = k.shape[0]
    return call(
        state_kernel,
        jax.ShapeDtypeStruct((H, DH, DH), BF16),
        (H // HB,),
        [columns(tokens), columns(tokens)],
        per_head(),
        flops=2 * tokens * D * DH,
        moved=6 * tokens * D,
    )(k, v)


def running_kernel(backwards, in_ref, out_ref):
    n = in_ref.shape[0]
    total = jnp.zeros(in_ref.shape[1:], F32)
    for i in reversed(range(n)) if backwards else range(n):
        out_ref[i] = total.astype(BF16)
        total += in_ref[i].astype(F32)


def running_sum(terms, backwards):
    n = lax.axis_size("ctx")
    parts = terms.reshape(n, H // n * DH, DH)
    here = lax.all_to_all(parts, "ctx", split_axis=0, concat_axis=0, tiled=True)
    sums = call(
        functools.partial(running_kernel, backwards),
        jax.ShapeDtypeStruct(here.shape, BF16),
        (1,),
        [whole(here.shape)],
        whole(here.shape),
        flops=here.size,
        moved=4 * here.size,
    )(here)
    back = lax.all_to_all(sums, "ctx", split_axis=0, concat_axis=0, tiled=True)
    return back.reshape(H, DH, DH)


def forward_kernel(
    q_ref, k_ref, v_ref, prior_ref, earlier_ref, gain_ref, router_ref, chosen_ref, pick_ref,
    z_ref, att_ref, sig_ref, send_ref, logits_ref,
):
    tokens = q_ref.shape[0]
    causal = causal_mask(tokens)
    step = pl.program_id(0)

    @pl.when(step == 0)
    def _():
        logits_ref[...] = jnp.zeros_like(logits_ref)

    for h in range(HB):
        q, k, v = q_ref[:, head(h)], k_ref[:, head(h)], v_ref[:, head(h)]
        high, low = halves(prior_ref[h] + earlier_ref[h].astype(F32))
        scores = jnp.where(causal, mm_nt(q, k), 0.0).astype(BF16)
        att = mm(scores, v) + mm(q, high) + mm(q, low)
        mean = jnp.mean(att * att, axis=1, keepdims=True)
        z = (att / jnp.sqrt(mean + EPS) * gain_ref[:, head(h)]).astype(BF16)
        att_ref[:, head(h)] = att
        z_ref[:, head(h)] = z
    z = z_ref[...]
    logits_ref[...] += mm(z, router_ref[...])
    send_ref[...] = mm(pick_ref[...], z).astype(BF16)

    @pl.when(step == pl.num_programs(0) - 1)
    def _():
        sig_ref[...] = jax.nn.sigmoid(logits_ref[...]) * chosen_ref[...]


def attention_forward(q, k, v, prior, earlier, gain, router, chosen, pick):
    tokens, rows, experts = q.shape[0], pick.shape[0], router.shape[1]
    return call(
        forward_kernel,
        (
            jax.ShapeDtypeStruct((tokens, D), BF16),
            jax.ShapeDtypeStruct((tokens, D), F32),
            jax.ShapeDtypeStruct((tokens, experts), F32),
            jax.ShapeDtypeStruct((rows, D), BF16),
        ),
        (H // HB,),
        [
            columns(tokens),
            columns(tokens),
            columns(tokens),
            per_head(),
            per_head(),
            columns(1),
            pl.BlockSpec((WIDTH, experts), lambda i: (i, 0)),
            whole((tokens, experts)),
            whole((rows, tokens)),
        ],
        (columns(tokens), columns(tokens), whole((tokens, experts)), columns(rows)),
        scratch=[pltpu.VMEM((tokens, experts), F32)],
        flops=2 * tokens * D * (4 * DH + rows),
        moved=2 * D * (8 * tokens + rows),
    )(q, k, v, prior, earlier, gain, router, chosen, pick)


def middle_kernel(
    q_ref, z_ref, att_ref, dy_ref, back_ref, pick_ref, dg_ref, sig_ref, gain_ref, router_ref,
    datt_ref, term_ref, rterm_ref, dlog_ref,
):
    experts = sig_ref.shape[1]

    @pl.when(pl.program_id(0) == 0)
    def _():
        sig = sig_ref[...]
        both = mm_tn(pick_ref[...], dg_ref[...])
        dg = both[:, :experts] + both[:, experts:]
        total = jnp.sum(sig, axis=1, keepdims=True)
        mean = jnp.sum(sig * dg, axis=1, keepdims=True) / total
        dlog = sig * (1.0 - sig) * (dg - mean) / total
        for i, part in enumerate(thirds(dlog)):
            dlog_ref[i] = part

    z, router = z_ref[...], router_ref[...]
    dz = dy_ref[...].astype(F32) + mm_tn(pick_ref[...], back_ref[...])
    term = jnp.zeros(rterm_ref.shape, F32)
    for i in range(3):
        dlog = dlog_ref[i]
        dz += mm_nt(dlog, router)
        term += mm_tn(dlog, z)
    rterm_ref[...] = term
    weighted = dz * gain_ref[...]
    for h in range(HB):
        att, w = att_ref[:, head(h)], weighted[:, head(h)]
        mean = jnp.mean(att * att, axis=1, keepdims=True) + EPS
        inner = jnp.sum(w * att, axis=1, keepdims=True)
        datt = ((w - att * (inner / (DH * mean))) / jnp.sqrt(mean)).astype(BF16)
        datt_ref[:, head(h)] = datt
        term_ref[h] = mm_tn(q_ref[:, head(h)], datt).astype(BF16)


def attention_middle(q, z, att, dy, back, pick, dg, sig, gain, router):
    tokens, rows, experts = q.shape[0], pick.shape[0], router.shape[1]
    return call(
        middle_kernel,
        (
            jax.ShapeDtypeStruct((tokens, D), BF16),
            jax.ShapeDtypeStruct((H, DH, DH), BF16),
            jax.ShapeDtypeStruct((experts, D), F32),
        ),
        (H // HB,),
        [
            columns(tokens),
            columns(tokens),
            columns(tokens),
            columns(tokens),
            columns(rows),
            whole((rows, tokens)),
            whole((rows, 2 * experts)),
            whole((tokens, experts)),
            columns(1),
            pl.BlockSpec((WIDTH, experts), lambda i: (i, 0)),
        ],
        (columns(tokens), per_head(), columns(experts)),
        scratch=[pltpu.VMEM((3, tokens, experts), BF16)],
        flops=2 * tokens * D * (DH + rows + 6 * experts),
        moved=2 * D * (8 * tokens + rows),
    )(q, z, att, dy, back, pick, dg, sig, gain, router)


def early_kernel(q_ref, k_ref, v_ref, datt_ref, prior_ref, earlier_ref, gq_ref, gk_ref, gv_ref):
    causal = causal_mask(q_ref.shape[0])
    for h in range(HB):
        q, k, v = q_ref[:, head(h)], k_ref[:, head(h)], v_ref[:, head(h)]
        datt = datt_ref[:, head(h)]
        high, low = halves(prior_ref[h] + earlier_ref[h].astype(F32))
        dscores = jnp.where(causal, mm_nt(datt, v), 0.0).astype(BF16)
        scores = jnp.where(causal, mm_nt(q, k), 0.0).astype(BF16)
        gq = mm(dscores, k) + mm_nt(datt, high) + mm_nt(datt, low)
        gq_ref[:, head(h)] = gq.astype(BF16)
        gk_ref[:, head(h)] = mm_tn(dscores, q)
        gv_ref[:, head(h)] = mm_tn(scores, datt)


def attention_early(q, k, v, datt, prior, earlier):
    tokens = q.shape[0]
    block = columns(tokens)
    return call(
        early_kernel,
        (
            jax.ShapeDtypeStruct((tokens, D), BF16),
            jax.ShapeDtypeStruct((tokens, D), F32),
            jax.ShapeDtypeStruct((tokens, D), F32),
        ),
        (H // HB,),
        [block, block, block, block, per_head(), per_head()],
        (block, block, block),
        flops=2 * tokens * D * DH * 7,
        moved=22 * D * tokens,
    )(q, k, v, datt, prior, earlier)


def late_kernel(k_ref, v_ref, later_ref, gk_ref, gv_ref, out_k_ref, out_v_ref):
    for h in range(HB):
        later = later_ref[h]
        out_k_ref[:, head(h)] = (gk_ref[:, head(h)] + mm_nt(v_ref[:, head(h)], later)).astype(BF16)
        out_v_ref[:, head(h)] = (gv_ref[:, head(h)] + mm(k_ref[:, head(h)], later)).astype(BF16)


def attention_late(k, v, later, gk, gv):
    tokens = k.shape[0]
    block = columns(tokens)
    out = jax.ShapeDtypeStruct((tokens, D), BF16)
    return call(
        late_kernel,
        (out, out),
        (H // HB,),
        [block, block, per_head(), block, block],
        (block, block),
        flops=2 * tokens * D * DH * 2,
        moved=18 * D * tokens,
    )(k, v, later, gk, gv)


def output_kernel(z_ref, pick_ref, back_ref, out_ref):
    out_ref[...] = (z_ref[...].astype(F32) + mm_tn(pick_ref[...], back_ref[...])).astype(BF16)


def layer_output(z, pick, back):
    tokens, rows = z.shape[0], pick.shape[0]
    return call(
        output_kernel,
        jax.ShapeDtypeStruct((tokens, D), BF16),
        (D // WIDTH,),
        [columns(tokens), whole((rows, tokens)), columns(rows)],
        columns(tokens),
        flops=2 * tokens * D * rows,
        moved=2 * D * rows,
    )(z, pick, back)


def exchange(rows, experts):
    shaped = rows.reshape(experts, rows.shape[0] // experts, rows.shape[1])
    moved = lax.all_to_all(shaped, ALL, split_axis=0, concat_axis=0, tiled=True)
    return moved.reshape(rows.shape)


def local(
    queries,
    keys,
    values,
    prior_state,
    norm_gain,
    router_weight,
    expert_ids,
    w_gate,
    w_up,
    w_down,
    cotangent,
):
    q, k, v, dy = queries[0], keys[0], values[0], cotangent[0]
    tokens = q.shape[0]
    experts = router_weight.shape[1]
    cap = max(2, 3 * tokens * TOPK // (2 * experts))
    gate_mat, up_mat, down_mat = w_gate[0], w_up[0], w_down[0]
    prior = prior_state[0]
    gain = norm_gain.reshape(1, D)
    me = lax.axis_index(ALL)

    terms = state_terms(k, v)
    pick, chosen, mask_send, dy_send = route(expert_ids[0], dy, experts, cap)
    earlier = running_sum(terms, False)
    mask_rows = exchange(mask_send, experts)
    dy_rows = exchange(dy_send, experts)
    z, att, sig, z_send = attention_forward(
        q, k, v, prior, earlier, gain, router_weight, chosen, pick
    )
    z_rows = exchange(z_send, experts)

    dh_plain = mm_nt(dy_rows, down_mat)
    sig_rows = jax.nn.sigmoid(mm(z_rows, router_weight)) * mask_rows.astype(F32)
    total = jnp.sum(sig_rows, axis=1, keepdims=True)
    lane = lax.broadcasted_iota(jnp.int32, sig_rows.shape, 1)
    mine = jnp.sum(jnp.where(lane == me, sig_rows, 0.0), axis=1, keepdims=True)
    gate = jnp.where(total > 0, mine / jnp.where(total > 0, total, 1.0), 0.0)
    gp = mm(z_rows, gate_mat)
    up = mm(z_rows, up_mat)
    gs = jax.nn.sigmoid(gp)
    hid = (gp * gs * up).astype(BF16)
    eo = mm(hid, down_mat)
    dg = jnp.sum(dy_rows.astype(F32) * eo, axis=1, keepdims=True)
    dg_high = lax.reduce_precision(dg, 8, 7)
    dg_low = dg - dg_high
    wide = lax.broadcasted_iota(jnp.int32, (z_rows.shape[0], 2 * experts), 1)
    dg_send = jnp.where(
        wide == me, dg_high, jnp.where(wide == me + experts, dg_low, 0.0)
    ).astype(BF16)
    eo_send = (gate * eo).astype(BF16)
    dg_back = exchange(dg_send, experts)
    dh = dh_plain * gate
    dgp = (dh * up * gs * (1.0 + gp * (1.0 - gs))).astype(BF16)
    dup = (dh * gp * gs).astype(BF16)
    dz_send = (gate * (mm_nt(dgp, gate_mat) + mm_nt(dup, up_mat))).astype(BF16)
    dz_back = exchange(dz_send, experts)
    eo_back = exchange(eo_send, experts)
    de = (gate * dy_rows.astype(F32)).astype(BF16)
    grad_down = mm_tn(hid, de).astype(BF16)
    grad_gate = mm_tn(z_rows, dgp).astype(BF16)
    grad_up = mm_tn(z_rows, dup).astype(BF16)

    datt, dterms, rterm = attention_middle(
        q, z, att, dy, dz_back, pick, dg_back, sig, gain, router_weight
    )
    later = running_sum(dterms, True)
    gq, gk, gv = attention_early(q, k, v, datt, prior, earlier)
    grad_k, grad_v = attention_late(k, v, later, gk, gv)
    output = layer_output(z, pick, eo_back)

    parts = rterm.reshape(experts, D // DH, DH)
    ours = lax.all_to_all(parts, ALL, split_axis=0, concat_axis=0, tiled=True)
    summed = jnp.sum(ours, axis=0, keepdims=True)
    spread = jnp.broadcast_to(summed, parts.shape)
    grad_router = lax.all_to_all(spread, ALL, split_axis=0, concat_axis=0, tiled=True)
    grad_router = grad_router.reshape(experts, D).T
    return (
        output[None],
        gq[None],
        grad_k[None],
        grad_v[None],
        grad_gate[None],
        grad_up[None],
        grad_down[None],
        grad_router,
    )


def solution(mesh):
    tokens = P("dp", "ctx", None)
    weights = P(ALL, None, None)
    placed = (
        tokens,
        tokens,
        tokens,
        P("dp", None, None, None),
        P(),
        P(),
        tokens,
        weights,
        weights,
        weights,
        tokens,
    )
    return jax.shard_map(
        local,
        mesh=mesh,
        in_specs=placed,
        out_specs=(tokens, tokens, tokens, tokens, weights, weights, weights, P()),
        check_vma=False,
    )
```

```python
import functools

import jax
import jax.numpy as jnp
from jax import lax
from jax.experimental import pallas as pl
from jax.experimental.pallas import tpu as pltpu
from jax.sharding import Mesh
from jax.sharding import PartitionSpec as P

H = 16
DH = 128
D = 2048
TOPK = 4
HB = 8
WIDTH = 512
HEADS = HB * DH
EPS = 1e-05
ALL = ("far", "near", "ctx")
F32 = jnp.float32
BF16 = jnp.bfloat16
LIMIT = 60 << 20


def mm(a, b):
    return jnp.dot(a, b, preferred_element_type=F32)


def mm_tn(a, b):
    return lax.dot_general(a, b, (((0,), (0,)), ((), ())), preferred_element_type=F32)


def mm_nt(a, b):
    return lax.dot_general(a, b, (((1,), (1,)), ((), ())), preferred_element_type=F32)


def halves(x):
    high = x.astype(BF16)
    return high, (x - high.astype(F32)).astype(BF16)


def thirds(x):
    high, rest = x.astype(BF16), None
    rest = x - high.astype(F32)
    middle = rest.astype(BF16)
    return high, middle, (rest - middle.astype(F32)).astype(BF16)


def causal_mask(n):
    return lax.broadcasted_iota(jnp.int32, (n, n), 0) >= lax.broadcasted_iota(jnp.int32, (n, n), 1)


def head(h):
    return slice(h * DH, (h + 1) * DH)


def call(kernel, out_shape, grid, in_specs, out_specs, scratch=(), flops=0, moved=0):
    return pl.pallas_call(
        kernel,
        out_shape=out_shape,
        grid=grid,
        in_specs=in_specs,
        out_specs=out_specs,
        scratch_shapes=scratch,
        compiler_params=pltpu.CompilerParams(vmem_limit_bytes=LIMIT),
        cost_estimate=pl.CostEstimate(flops=flops, bytes_accessed=moved, transcendentals=0),
    )


def whole(shape):
    return pl.BlockSpec(shape, lambda *_: (0,) * len(shape))


def columns(rows, width=HEADS):
    return pl.BlockSpec((rows, width), lambda i: (0, i))


def per_head(n=HB):
    return pl.BlockSpec((n, DH, DH), lambda i: (i, 0, 0))


def lanes_of(n):
    return -(-n // 128) * 128


def route_kernel(cap, top, plane_ref, *refs):
    *ids_refs, pick_ref, chosen_ref = refs
    tokens = ids_refs[0].shape[0]
    experts = chosen_ref.shape[1]
    rows = pick_ref.shape[0]
    slots = len(ids_refs) * cap
    group = rows // slots
    row = lax.broadcasted_iota(jnp.int32, (rows, experts), 0)
    first = lax.broadcasted_iota(jnp.int32, (rows, experts), 1) - plane_ref[0, 0] * group
    first = first * slots
    owns = (row >= first) & (row < first + slots)
    wanted = jnp.sum(jnp.where(owns, row - first + 1, 0), axis=1, keepdims=True).astype(F32)
    owns = owns.astype(F32).astype(BF16)
    lane = lax.broadcasted_iota(jnp.int32, (tokens, experts), 1)
    earlier = causal_mask(tokens).astype(F32).astype(BF16)
    for b, ref in enumerate(ids_refs):
        ids = ref[...].astype(F32)
        chosen = jnp.zeros((tokens, experts), F32)
        for j in range(top):
            chosen += (ids[:, j : j + 1] == lane.astype(F32)).astype(F32)
        place = chosen * (mm(earlier, chosen.astype(BF16)) + float(b * cap))
        found = mm_nt(owns, place.astype(BF16))
        at = slice(b * tokens, (b + 1) * tokens)
        pick_ref[:, at] = (found == wanted).astype(F32).astype(BF16)
        chosen_ref[at] = chosen


def smem():
    return pl.BlockSpec(memory_space=pltpu.SMEM)


def route(plane, blocks, experts, rows, cap):
    tokens, n = blocks[0].shape[0], len(blocks)
    return call(
        functools.partial(route_kernel, cap, TOPK),
        (
            jax.ShapeDtypeStruct((rows, n * tokens), BF16),
            jax.ShapeDtypeStruct((n * tokens, experts), F32),
        ),
        (1,),
        [smem()] + [pl.BlockSpec((tokens, 128), lambda i: (0, D // 128))] * n,
        (whole((rows, n * tokens)), whole((n * tokens, experts))),
        flops=2 * n * rows * tokens * experts,
        moved=2 * n * rows * tokens,
    )(plane, *blocks)


def gather_kernel(masked, pick_ref, chosen_ref, *refs):
    *block_refs, send_ref, stack_ref = refs
    tokens = block_refs[0].shape[0]
    pick = pick_ref[...]
    for b, ref in enumerate(block_refs):
        stack_ref[b * tokens : (b + 1) * tokens] = ref[:, :D]
    for c in range(D // WIDTH):
        at = slice(c * WIDTH, (c + 1) * WIDTH)
        send_ref[:, at] = mm(pick, stack_ref[:, at]).astype(BF16)
    if masked:
        experts = chosen_ref.shape[1]
        if send_ref.shape[1] > D + experts:
            send_ref[:, D:] = jnp.zeros((send_ref.shape[0], send_ref.shape[1] - D), BF16)
        mask = mm(pick, chosen_ref[...].astype(BF16))
        send_ref[:, D : D + experts] = mask.astype(BF16)


def gather(pick, chosen, blocks, masked):
    rows = pick.shape[0]
    width = D + (lanes_of(chosen.shape[1]) if masked else 0)
    return call(
        functools.partial(gather_kernel, masked),
        jax.ShapeDtypeStruct((rows, width), BF16),
        (1,),
        [whole(pick.shape), whole(chosen.shape)] + [whole(blocks[0].shape)] * len(blocks),
        whole((rows, width)),
        scratch=[pltpu.VMEM((pick.shape[1], D), BF16)],
        flops=2 * rows * pick.shape[1] * D,
        moved=2 * rows * D,
    )(pick, chosen, *blocks)


def partial_kernel(pick_ref, back_ref, *out_refs):
    tokens, width = out_refs[0].shape
    for b, ref in enumerate(out_refs):
        pick = pick_ref[:, (b + 1) * tokens : (b + 2) * tokens]
        for c in range(0, width, WIDTH):
            at = slice(c, min(c + WIDTH, width))
            ref[:, at] = mm_tn(pick, back_ref[:, at]).astype(BF16)


def partials(pick, back, tokens):
    others = pick.shape[1] // tokens - 1
    rows, width = back.shape
    return call(
        partial_kernel,
        (jax.ShapeDtypeStruct((tokens, width), BF16),) * others,
        (1,),
        [whole(pick.shape), whole(back.shape)],
        (whole((tokens, width)),) * others,
        flops=2 * others * rows * width * tokens,
        moved=2 * rows * width,
    )(pick, back)


def state_kernel(k_ref, v_ref, out_ref):
    for h in range(HB):
        out_ref[h] = mm_tn(k_ref[:, head(h)], v_ref[:, head(h)]).astype(BF16)


def state_terms(k, v):
    tokens = k.shape[0]
    return call(
        state_kernel,
        jax.ShapeDtypeStruct((H, DH, DH), BF16),
        (H // HB,),
        [columns(tokens), columns(tokens)],
        per_head(),
        flops=2 * tokens * D * DH,
        moved=6 * tokens * D,
    )(k, v)


def running_kernel(backwards, states, in_ref, out_ref):
    n, rows, _ = in_ref.shape
    total = jnp.zeros((states, DH), F32)
    for i in reversed(range(n)) if backwards else range(n):
        out_ref[i, :states] = total.astype(BF16)
        total += in_ref[i, :states].astype(F32)
    if rows > states:
        half = (rows - states) // 2
        whole_sum = jnp.zeros((half, DH), F32)
        for i in range(n):
            whole_sum += in_ref[i, states : states + half].astype(F32)
            whole_sum += in_ref[i, states + half :].astype(F32)
        high, low = halves(whole_sum)
        for i in range(n):
            out_ref[i, states : states + half] = high
            out_ref[i, states + half :] = low


def to_heads(block):
    return lax.all_to_all(block, "ctx", split_axis=0, concat_axis=0, tiled=True)


def running_sum(here, backwards):
    states = H // here.shape[0] * DH
    return call(
        functools.partial(running_kernel, backwards, states),
        jax.ShapeDtypeStruct(here.shape, BF16),
        (1,),
        [whole(here.shape)],
        whole(here.shape),
        flops=here.size,
        moved=4 * here.size,
    )(here)


def forward_kernel(
    q_ref, k_ref, v_ref, prior_ref, earlier_ref, gain_ref, router_ref, ids_ref,
    z_ref, att_ref, sig_ref, logits_ref,
):
    tokens = q_ref.shape[0]
    causal = causal_mask(tokens)
    step = pl.program_id(0)

    @pl.when(step == 0)
    def _():
        logits_ref[...] = jnp.zeros_like(logits_ref)

    for h in range(HB):
        q, k, v = q_ref[:, head(h)], k_ref[:, head(h)], v_ref[:, head(h)]
        high, low = halves(prior_ref[h] + earlier_ref[h].astype(F32))
        scores = jnp.where(causal, mm_nt(q, k), 0.0).astype(BF16)
        att = mm(scores, v) + mm(q, high) + mm(q, low)
        mean = jnp.mean(att * att, axis=1, keepdims=True)
        z = (att / jnp.sqrt(mean + EPS) * gain_ref[:, head(h)]).astype(BF16)
        att_ref[:, head(h)] = att
        z_ref[:, head(h)] = z
    logits_ref[...] += mm(z_ref[...], router_ref[...])

    @pl.when(step == pl.num_programs(0) - 1)
    def _():
        experts = sig_ref.shape[1]
        lane = lax.broadcasted_iota(jnp.int32, (tokens, experts), 1)
        chosen = jnp.zeros((tokens, experts), F32)
        for j in range(ids_ref.shape[1]):
            chosen += (ids_ref[:, j : j + 1] == lane).astype(F32)
        sig_ref[...] = jax.nn.sigmoid(logits_ref[...]) * chosen


def attention_forward(q, k, v, prior, earlier, gain, router, ids):
    tokens, experts = q.shape[0], router.shape[1]
    return call(
        forward_kernel,
        (
            jax.ShapeDtypeStruct((tokens, D), BF16),
            jax.ShapeDtypeStruct((tokens, D), F32),
            jax.ShapeDtypeStruct((tokens, experts), F32),
        ),
        (H // HB,),
        [
            columns(tokens),
            columns(tokens),
            columns(tokens),
            per_head(),
            per_head(),
            columns(1),
            pl.BlockSpec((HEADS, experts), lambda i: (i, 0)),
            whole(ids.shape),
        ],
        (columns(tokens), columns(tokens), whole((tokens, experts))),
        scratch=[pltpu.VMEM((tokens, experts), F32)],
        flops=2 * tokens * D * 4 * DH,
        moved=2 * D * 8 * tokens,
    )(q, k, v, prior, earlier, gain, router, ids)


def router_kernel(*refs):
    z_ref, dg_ref, pick_ref, sig_ref, *more_refs, dlog_ref, term_ref = refs
    tokens, experts = sig_ref.shape

    @pl.when(pl.program_id(0) == 0)
    def _():
        sig = sig_ref[...]
        both = mm_tn(pick_ref[:, :tokens], dg_ref[...])
        for ref in more_refs:
            both += ref[...].astype(F32)
        dg = both[:, :experts] + both[:, experts : 2 * experts]
        total = jnp.sum(sig, axis=1, keepdims=True)
        mean = jnp.sum(sig * dg, axis=1, keepdims=True) / total
        dlog = sig * (1.0 - sig) * (dg - mean) / total
        for i, part in enumerate(thirds(dlog)):
            dlog_ref[i] = part

    z = z_ref[...]
    term_ref[...] = mm_tn(dlog_ref[0], z) + mm_tn(dlog_ref[1], z) + mm_tn(dlog_ref[2], z)


def router_gradient(z, back, more, pick, sig):
    tokens, experts = sig.shape
    rows = pick.shape[0]
    wide = lanes_of(2 * experts)
    return call(
        router_kernel,
        (
            jax.ShapeDtypeStruct((3, tokens, experts), BF16),
            jax.ShapeDtypeStruct((experts, D), F32),
        ),
        (D // WIDTH,),
        [
            columns(tokens, WIDTH),
            whole((rows, wide)),
            whole(pick.shape),
            whole(sig.shape),
        ]
        + [whole((tokens, wide))] * len(more),
        (whole((3, tokens, experts)), columns(experts, WIDTH)),
        flops=6 * tokens * experts * D,
        moved=2 * tokens * D,
    )(z, back, pick, sig, *more)


def middle_kernel(*refs):
    q_ref, att_ref, dy_ref, back_ref, pick_ref, dlog_ref, gain_ref, router_ref, rterm_ref = refs[:9]
    *more_refs, datt_ref, term_ref = refs[9:]
    experts = router_ref.shape[1]
    per = HB // term_ref.shape[0]
    tokens = q_ref.shape[0]
    router = router_ref[...]
    dz = dy_ref[...].astype(F32) + mm_tn(pick_ref[:, :tokens], back_ref[...])
    for ref in more_refs:
        dz += ref[...].astype(F32)
    for i in range(3):
        dz += mm_nt(dlog_ref[i], router)
    weighted = dz * gain_ref[...]
    for h in range(HB):
        att, w = att_ref[:, head(h)], weighted[:, head(h)]
        mean = jnp.mean(att * att, axis=1, keepdims=True) + EPS
        inner = jnp.sum(w * att, axis=1, keepdims=True)
        datt = ((w - att * (inner / (DH * mean))) / jnp.sqrt(mean)).astype(BF16)
        datt_ref[:, head(h)] = datt
        to, i = h // per, h % per
        term_ref[to, head(i)] = mm_tn(q_ref[:, head(h)], datt).astype(BF16)
        high, low = halves(rterm_ref[:, head(h)])
        at = per * DH + i * experts
        term_ref[to, at : at + experts] = high
        term_ref[to, at + per * experts : at + per * experts + experts] = low


def attention_middle(q, att, dy, back, more, pick, dlog, gain, router, rterm, n):
    tokens, rows, experts = q.shape[0], pick.shape[0], router.shape[1]
    per = H // n
    length = per * (DH + 2 * experts)
    return call(
        middle_kernel,
        (
            jax.ShapeDtypeStruct((tokens, D), BF16),
            jax.ShapeDtypeStruct((n, length, DH), BF16),
        ),
        (H // HB,),
        [
            columns(tokens),
            columns(tokens),
            columns(tokens),
            columns(rows),
            whole(pick.shape),
            whole(dlog.shape),
            columns(1),
            pl.BlockSpec((HEADS, experts), lambda i: (i, 0)),
            columns(experts),
        ]
        + [columns(tokens)] * len(more),
        (columns(tokens), pl.BlockSpec((HB // per, length, DH), lambda i: (i, 0, 0))),
        flops=2 * tokens * D * (DH + rows + 3 * experts),
        moved=2 * D * (8 * tokens + rows),
    )(q, att, dy, back, pick, dlog, gain, router, rterm, *more)


def early_kernel(q_ref, k_ref, v_ref, datt_ref, prior_ref, earlier_ref, gq_ref, gk_ref, gv_ref):
    causal = causal_mask(q_ref.shape[0])
    for h in range(HB):
        q, k, v = q_ref[:, head(h)], k_ref[:, head(h)], v_ref[:, head(h)]
        datt = datt_ref[:, head(h)]
        high, low = halves(prior_ref[h] + earlier_ref[h].astype(F32))
        dscores = jnp.where(causal, mm_nt(datt, v), 0.0).astype(BF16)
        scores = jnp.where(causal, mm_nt(q, k), 0.0).astype(BF16)
        gq = mm(dscores, k) + mm_nt(datt, high) + mm_nt(datt, low)
        gq_ref[:, head(h)] = gq.astype(BF16)
        gk_ref[:, head(h)] = mm_tn(dscores, q)
        gv_ref[:, head(h)] = mm_tn(scores, datt)


def attention_early(q, k, v, datt, prior, earlier):
    tokens = q.shape[0]
    block = columns(tokens)
    return call(
        early_kernel,
        (
            jax.ShapeDtypeStruct((tokens, D), BF16),
            jax.ShapeDtypeStruct((tokens, D), F32),
            jax.ShapeDtypeStruct((tokens, D), F32),
        ),
        (H // HB,),
        [block, block, block, block, per_head(), per_head()],
        (block, block, block),
        flops=2 * tokens * D * DH * 7,
        moved=22 * D * tokens,
    )(q, k, v, datt, prior, earlier)


def late_kernel(k_ref, v_ref, later_ref, gk_ref, gv_ref, out_k_ref, out_v_ref, router_ref):
    experts = router_ref.shape[1]
    per = HB // later_ref.shape[0]
    for h in range(HB):
        to, i = h // per, h % per
        later = later_ref[to, head(i)]
        out_k_ref[:, head(h)] = (gk_ref[:, head(h)] + mm_nt(v_ref[:, head(h)], later)).astype(BF16)
        out_v_ref[:, head(h)] = (gv_ref[:, head(h)] + mm(k_ref[:, head(h)], later)).astype(BF16)
        at = per * DH + i * experts
        high = later_ref[to, at : at + experts].astype(F32)
        low = later_ref[to, at + per * experts : at + per * experts + experts].astype(F32)
        router_ref[head(h)] = (high + low).T


def attention_late(k, v, later, gk, gv, experts):
    tokens = k.shape[0]
    block = columns(tokens)
    out = jax.ShapeDtypeStruct((tokens, D), BF16)
    n, length, _ = later.shape
    return call(
        late_kernel,
        (out, out, jax.ShapeDtypeStruct((D, experts), F32)),
        (H // HB,),
        [
            block,
            block,
            pl.BlockSpec((HB * n // H, length, DH), lambda i: (i, 0, 0)),
            block,
            block,
        ],
        (block, block, pl.BlockSpec((HEADS, experts), lambda i: (i, 0))),
        flops=2 * tokens * D * DH * 2,
        moved=18 * D * tokens,
    )(k, v, later, gk, gv)


def output_kernel(z_ref, pick_ref, back_ref, *refs):
    *more_refs, out_ref = refs
    tokens = z_ref.shape[0]
    total = z_ref[...].astype(F32) + mm_tn(pick_ref[:, :tokens], back_ref[...])
    for ref in more_refs:
        total += ref[...].astype(F32)
    out_ref[...] = total.astype(BF16)


def layer_output(z, pick, back, more):
    tokens, rows = z.shape[0], pick.shape[0]
    return call(
        output_kernel,
        jax.ShapeDtypeStruct((tokens, D), BF16),
        (D // HEADS,),
        [columns(tokens), whole(pick.shape), columns(rows)] + [columns(tokens)] * len(more),
        columns(tokens),
        flops=2 * tokens * D * rows,
        moved=2 * D * rows,
    )(z, pick, back, *more)


def down_kernel(dy_ref, down_ref, out_ref):
    out_ref[...] = mm_nt(dy_ref[...], down_ref[...])


def expert_down_back(dy_rows, down_mat):
    rows, hidden = dy_rows.shape[0], down_mat.shape[0]
    tile = 256
    return call(
        down_kernel,
        jax.ShapeDtypeStruct((rows, hidden), F32),
        (hidden // tile,),
        [
            pl.BlockSpec((rows, D), lambda i: (0, 0)),
            pl.BlockSpec((tile, D), lambda i: (i, 0)),
        ],
        columns(rows, tile),
        flops=2 * rows * hidden * D,
        moved=2 * (rows + hidden) * D,
    )(dy_rows, down_mat)


def expert_kernel(
    me_ref, z_ref, mask_ref, router_ref, gate_ref, up_ref, dh_ref,
    hid_ref, dgp_ref, dup_ref, weight_ref, pair_ref, dg_ref,
):
    experts = router_ref.shape[1]

    @pl.when(pl.program_id(0) == 0)
    def _():
        sig = jax.nn.sigmoid(mm(z_ref[...], router_ref[...]))
        sig *= mask_ref[:, :experts].astype(F32)
        total = jnp.sum(sig, axis=1, keepdims=True)
        lane = lax.broadcasted_iota(jnp.int32, sig.shape, 1)
        mine = jnp.sum(jnp.where(lane == me_ref[0, 0], sig, 0.0), axis=1, keepdims=True)
        some = total > 0
        weight_ref[...] = jnp.where(some, mine / jnp.where(some, total, 1.0), 0.0)
        dg_ref[...] = jnp.zeros_like(dg_ref)

    z = z_ref[...]
    gp = mm(z, gate_ref[...])
    up = mm(z, up_ref[...])
    gs = jax.nn.sigmoid(gp)
    hid = (gp * gs * up).astype(BF16)
    plain = dh_ref[...]
    dg_ref[...] += jnp.sum(plain * hid.astype(F32), axis=1, keepdims=True)
    dh = plain * weight_ref[...]
    hid_ref[...] = hid
    dgp_ref[...] = (dh * up * gs * (1.0 + gp * (1.0 - gs))).astype(BF16)
    dup_ref[...] = (dh * gp * gs).astype(BF16)

    @pl.when(pl.program_id(0) == pl.num_programs(0) - 1)
    def _():
        lane = lax.broadcasted_iota(jnp.int32, pair_ref.shape, 1)
        dg = dg_ref[...]
        high = dg.astype(BF16).astype(F32)
        pair = jnp.where(lane == me_ref[0, 0], high, 0.0)
        pair = jnp.where(lane == me_ref[0, 0] + experts, dg - high, pair)
        pair_ref[...] = pair.astype(BF16)


def expert_forward(me, z_rows, dy_rows, router, gate_mat, up_mat, dh_plain):
    rows, hidden, experts = z_rows.shape[0], gate_mat.shape[1], router.shape[1]
    tile, wide = 256, lanes_of(experts)
    beside = D // wide
    inner = jax.ShapeDtypeStruct((rows, hidden), BF16)
    column = jax.ShapeDtypeStruct((rows, 1), F32)
    pair = jax.ShapeDtypeStruct((rows, lanes_of(2 * experts)), BF16)
    return call(
        expert_kernel,
        (inner, inner, inner, column, pair),
        (hidden // tile,),
        [
            smem(),
            whole((rows, D)),
            pl.BlockSpec((rows, wide), lambda i: (0, beside)),
            whole(router.shape),
            columns(D, tile),
            columns(D, tile),
            columns(rows, tile),
        ],
        (columns(rows, tile),) * 3 + (whole((rows, 1)), whole(pair.shape)),
        scratch=[pltpu.VMEM((rows, 1), F32)],
        flops=4 * rows * hidden * D,
        moved=2 * (rows + 2 * hidden) * D,
    )(me, z_rows, dy_rows, router, gate_mat, up_mat, dh_plain)


def back_kernel(dgp_ref, dup_ref, gate_ref, up_ref, weight_ref, out_ref):
    total = mm_nt(dgp_ref[...], gate_ref[...]) + mm_nt(dup_ref[...], up_ref[...])
    out_ref[...] = (total * weight_ref[...]).astype(BF16)


def expert_back(dgp, dup, gate_mat, up_mat, weight):
    rows, hidden = dgp.shape
    stripe = pl.BlockSpec((WIDTH, hidden), lambda i: (i, 0))
    return call(
        back_kernel,
        jax.ShapeDtypeStruct((rows, D), BF16),
        (D // WIDTH,),
        [whole(dgp.shape), whole(dup.shape), stripe, stripe, whole((rows, 1))],
        columns(rows, WIDTH),
        flops=4 * rows * hidden * D,
        moved=2 * (rows + 2 * hidden) * D,
    )(dgp, dup, gate_mat, up_mat, weight)


def product_kernel(hid_ref, down_ref, weight_ref, out_ref):
    out_ref[...] = (mm(hid_ref[...], down_ref[...]) * weight_ref[...]).astype(BF16)


def expert_product(hid, down_mat, weight):
    rows, hidden = hid.shape
    return call(
        product_kernel,
        jax.ShapeDtypeStruct((rows, D), BF16),
        (D // WIDTH,),
        [whole(hid.shape), columns(hidden, WIDTH), whole((rows, 1))],
        columns(rows, WIDTH),
        flops=2 * rows * hidden * D,
        moved=2 * (rows + hidden) * D,
    )(hid, down_mat, weight)


def weights_kernel(
    z_ref, dy_ref, hid_ref, dgp_ref, dup_ref, weight_ref, gate_ref, up_ref, down_ref
):
    z = z_ref[...]
    gate_ref[...] = mm_tn(z, dgp_ref[...]).astype(BF16)
    up_ref[...] = mm_tn(z, dup_ref[...]).astype(BF16)
    de = (dy_ref[...].astype(F32) * weight_ref[...]).astype(BF16)
    down_ref[...] = mm_tn(hid_ref[...], de).astype(BF16)


def expert_weights(z_rows, dy_rows, hid, dgp, dup, weight):
    rows, hidden = hid.shape
    stripe = pl.BlockSpec((WIDTH, hidden), lambda i: (i, 0))
    return call(
        weights_kernel,
        (
            jax.ShapeDtypeStruct((D, hidden), BF16),
            jax.ShapeDtypeStruct((D, hidden), BF16),
            jax.ShapeDtypeStruct((hidden, D), BF16),
        ),
        (D // WIDTH,),
        [columns(rows, WIDTH), columns(rows, WIDTH)] + [whole(hid.shape)] * 3 + [whole((rows, 1))],
        (stripe, stripe, columns(hidden, WIDTH)),
        flops=6 * rows * hidden * D,
        moved=2 * (2 * rows + 3 * hidden) * D,
    )(z_rows, dy_rows, hid, dgp, dup, weight)


def exchange(rows):
    group = lax.axis_size("ctx")
    shaped = rows.reshape(group, rows.shape[0] // group, rows.shape[1])
    moved = lax.all_to_all(shaped, "ctx", split_axis=0, concat_axis=0, tiled=True)
    return moved.reshape(rows.shape)


def after(value, *earlier):
    return lax.optimization_barrier((value, *earlier))[0]


def swap(block, axis, by=1):
    return lax.ppermute(block, axis, [(i, i ^ by) for i in range(lax.axis_size(axis))])


def peers():
    return [(b % 2, b // 2) for b in range(2 * lax.axis_size("near"))]


def replicate(block, *gate):
    far = swap(block, "far")
    near = range(1, lax.axis_size("near"))
    own = [swap(block, "near", n) for n in near]
    gated = after(far, *gate) if gate else far
    other = [swap(gated, "near", n) for n in near]
    return [block, far] + [x for pair in zip(own, other) for x in pair]


def collect_far(parts):
    far = parts[0]
    near = range(1, lax.axis_size("near"))
    if len(near):
        arrived = [swap(parts[2 * n], "near", n) for n in near]
        far = sum((a.astype(F32) for a in arrived), far.astype(F32)).astype(BF16)
    return far


def collect(parts, far):
    near = range(1, lax.axis_size("near"))
    return [swap(far, "far")] + [swap(parts[2 * n - 1], "near", n) for n in near]


def collect_small(parts):
    near = lax.axis_size("near")
    steps = peers()[1:]
    return [swap(part, ("far", "near"), f * near + n) for part, (f, n) in zip(parts, steps)]


def doublings():
    steps = []
    for axis in ("far", "near"):
        by = 1
        while by < lax.axis_size(axis):
            steps.append((axis, by))
            by *= 2
    return steps


def sum_over(term, steps, gate):
    for axis, by in steps:
        term = term + after(swap(term, axis, by), gate)
    return term


def local(
    queries,
    keys,
    values,
    prior_state,
    norm_gain,
    router_weight,
    expert_ids,
    w_gate,
    w_up,
    w_down,
    cotangent,
):
    q, k, v, dy = queries[0], keys[0], values[0], cotangent[0]
    tokens = q.shape[0]
    experts = router_weight.shape[1]
    cap = max(2, 3 * tokens * TOPK // (2 * experts))
    gate_mat, up_mat, down_mat = w_gate[0], w_up[0], w_down[0]
    prior = prior_state[0]
    gain = norm_gain.reshape(1, D)
    me = jnp.stack([lax.axis_index(ALL), jnp.int32(experts)]).reshape(1, 2).astype(jnp.int32)
    plane = lax.axis_index(("far", "near")).reshape(1, 1).astype(jnp.int32)
    rows = experts * cap

    n = lax.axis_size("ctx")
    ids = expert_ids[0]
    beside = jnp.pad(ids.astype(BF16), ((0, 0), (0, 128 - TOPK)))
    terms = state_terms(k, v).reshape(n, H // n * DH, DH)
    here = to_heads(terms)
    sums = running_sum(here, False)
    dy_blocks = replicate(jnp.concatenate([dy, beside], axis=1), sums)
    earlier = to_heads(sums).reshape(H, DH, DH)
    z, att, sig = attention_forward(q, k, v, prior, earlier, gain, router_weight, ids)
    z_blocks = replicate(z)
    pick, chosen = route(plane, after(dy_blocks, z), experts, rows, cap)
    dy_rows = exchange(gather(pick, chosen, dy_blocks, True))
    z_rows = exchange(gather(pick, chosen, z_blocks, False))

    dh_plain = expert_down_back(dy_rows, down_mat)
    hid, dgp, dup, weight, dg_send = expert_forward(
        me, z_rows, dy_rows, router_weight, gate_mat, up_mat, dh_plain
    )
    dg_back = exchange(dg_send)
    dz_send = expert_back(dgp, dup, gate_mat, up_mat, weight)
    dz_back = exchange(dz_send)
    dg_more = collect_small(partials(pick, after(dg_back, dz_send), tokens))
    dlog, rterm = router_gradient(z, dg_back, dg_more, pick, sig)
    eo_send = expert_product(after(hid, dlog), down_mat, weight)
    steps = doublings()
    rterm = sum_over(rterm, steps[:1], eo_send)
    grad_gate, grad_up, grad_down = expert_weights(
        after(z_rows, rterm), dy_rows, hid, dgp, dup, weight
    )
    rterm = sum_over(rterm, steps[1:], grad_gate)

    dz_parts = partials(pick, after(dz_back, rterm), tokens)
    dz_far = collect_far(dz_parts)
    dz_more = collect(dz_parts, dz_far)
    eo_back = exchange(after(eo_send, *dz_parts))
    eo_parts = partials(pick, after(eo_back, dz_far), tokens)
    datt, dterms = attention_middle(
        q, att, dy, dz_back, after(dz_more, *eo_parts), pick, dlog, gain, router_weight, rterm, n
    )
    there = to_heads(dterms)
    gq, gk, gv = attention_early(q, k, v, datt, prior, earlier)
    eo_more = collect(eo_parts, collect_far(eo_parts))
    later = to_heads(running_sum(there, True))
    grad_k, grad_v, grad_router = attention_late(k, v, later, gk, gv, experts)
    output = layer_output(z, pick, eo_back, eo_more)
    return (
        output[None],
        gq[None],
        grad_k[None],
        grad_v[None],
        grad_gate[None],
        grad_up[None],
        grad_down[None],
        grad_router,
    )


def solution(mesh):
    tokens = P(("far", "near"), "ctx", None)
    weights = P(ALL, None, None)
    split = Mesh(
        mesh.devices.reshape(2, mesh.shape["dp"] // 2, mesh.shape["ctx"]), ("far", "near", "ctx")
    )
    placed = (
        tokens,
        tokens,
        tokens,
        P(("far", "near"), None, None, None),
        P(),
        P(),
        tokens,
        weights,
        weights,
        weights,
        tokens,
    )
    return jax.shard_map(
        local,
        mesh=split,
        in_specs=placed,
        out_specs=(tokens, tokens, tokens, tokens, weights, weights, weights, P()),
        check_vma=False,
    )
```

```python
import functools

import jax
import jax.numpy as jnp
from jax import lax
from jax.experimental import pallas as pl
from jax.experimental.pallas import tpu as pltpu
from jax.sharding import Mesh
from jax.sharding import PartitionSpec as P

H = 16
DH = 128
D = 2048
TOPK = 4
HB = 8
WIDTH = 512
HEADS = HB * DH
EPS = 1e-05
ALL = ("far", "near", "ctx")
F32 = jnp.float32
BF16 = jnp.bfloat16
LIMIT = 60 << 20


def mm(a, b):
    return jnp.dot(a, b, preferred_element_type=F32)


def mm_tn(a, b):
    return lax.dot_general(a, b, (((0,), (0,)), ((), ())), preferred_element_type=F32)


def mm_nt(a, b):
    return lax.dot_general(a, b, (((1,), (1,)), ((), ())), preferred_element_type=F32)


def halves(x):
    high = x.astype(BF16)
    return high, (x - high.astype(F32)).astype(BF16)


def thirds(x):
    high, rest = x.astype(BF16), None
    rest = x - high.astype(F32)
    middle = rest.astype(BF16)
    return high, middle, (rest - middle.astype(F32)).astype(BF16)


def causal_mask(n):
    return lax.broadcasted_iota(jnp.int32, (n, n), 0) >= lax.broadcasted_iota(jnp.int32, (n, n), 1)


def head(h):
    return slice(h * DH, (h + 1) * DH)


def call(kernel, out_shape, grid, in_specs, out_specs, scratch=(), flops=0, moved=0):
    return pl.pallas_call(
        kernel,
        out_shape=out_shape,
        grid=grid,
        in_specs=in_specs,
        out_specs=out_specs,
        scratch_shapes=scratch,
        compiler_params=pltpu.CompilerParams(vmem_limit_bytes=LIMIT),
        cost_estimate=pl.CostEstimate(flops=flops, bytes_accessed=moved, transcendentals=0),
    )


def whole(shape):
    return pl.BlockSpec(shape, lambda *_: (0,) * len(shape))


def columns(rows, width=HEADS):
    return pl.BlockSpec((rows, width), lambda i: (0, i))


def per_head(n=HB):
    return pl.BlockSpec((n, DH, DH), lambda i: (i, 0, 0))


def lanes_of(n):
    return -(-n // 128) * 128


def route_kernel(cap, top, plane_ref, *refs):
    *ids_refs, pick_ref, chosen_ref = refs
    tokens = ids_refs[0].shape[0]
    experts = chosen_ref.shape[1]
    rows = pick_ref.shape[0]
    slots = len(ids_refs) * cap
    group = rows // slots
    row = lax.broadcasted_iota(jnp.int32, (rows, experts), 0)
    first = lax.broadcasted_iota(jnp.int32, (rows, experts), 1) - plane_ref[0, 0] * group
    first = first * slots
    owns = (row >= first) & (row < first + slots)
    wanted = jnp.sum(jnp.where(owns, row - first + 1, 0), axis=1, keepdims=True).astype(F32)
    owns = owns.astype(F32).astype(BF16)
    lane = lax.broadcasted_iota(jnp.int32, (tokens, experts), 1)
    earlier = causal_mask(tokens).astype(F32).astype(BF16)
    for b, ref in enumerate(ids_refs):
        ids = ref[...].astype(F32)
        chosen = jnp.zeros((tokens, experts), F32)
        for j in range(top):
            chosen += (ids[:, j : j + 1] == lane.astype(F32)).astype(F32)
        place = chosen * (mm(earlier, chosen.astype(BF16)) + float(b * cap))
        found = mm_nt(owns, place.astype(BF16))
        at = slice(b * tokens, (b + 1) * tokens)
        pick_ref[:, at] = (found == wanted).astype(F32).astype(BF16)
        chosen_ref[at] = chosen


def smem():
    return pl.BlockSpec(memory_space=pltpu.SMEM)


def route(plane, blocks, experts, rows, cap):
    tokens, n = blocks[0].shape[0], len(blocks)
    return call(
        functools.partial(route_kernel, cap, TOPK),
        (
            jax.ShapeDtypeStruct((rows, n * tokens), BF16),
            jax.ShapeDtypeStruct((n * tokens, experts), F32),
        ),
        (1,),
        [smem()] + [pl.BlockSpec((tokens, 128), lambda i: (0, D // 128))] * n,
        (whole((rows, n * tokens)), whole((n * tokens, experts))),
        flops=2 * n * rows * tokens * experts,
        moved=2 * n * rows * tokens,
    )(plane, *blocks)


def gather_kernel(masked, pick_ref, chosen_ref, *refs):
    *block_refs, send_ref, stack_ref = refs
    tokens = block_refs[0].shape[0]
    pick = pick_ref[...]
    for b, ref in enumerate(block_refs):
        stack_ref[b * tokens : (b + 1) * tokens] = ref[:, :D]
    for c in range(D // WIDTH):
        at = slice(c * WIDTH, (c + 1) * WIDTH)
        send_ref[:, at] = mm(pick, stack_ref[:, at]).astype(BF16)
    if masked:
        experts = chosen_ref.shape[1]
        if send_ref.shape[1] > D + experts:
            send_ref[:, D:] = jnp.zeros((send_ref.shape[0], send_ref.shape[1] - D), BF16)
        mask = mm(pick, chosen_ref[...].astype(BF16))
        send_ref[:, D : D + experts] = mask.astype(BF16)


def gather(pick, chosen, blocks, masked):
    rows = pick.shape[0]
    width = D + (lanes_of(chosen.shape[1]) if masked else 0)
    return call(
        functools.partial(gather_kernel, masked),
        jax.ShapeDtypeStruct((rows, width), BF16),
        (1,),
        [whole(pick.shape), whole(chosen.shape)] + [whole(blocks[0].shape)] * len(blocks),
        whole((rows, width)),
        scratch=[pltpu.VMEM((pick.shape[1], D), BF16)],
        flops=2 * rows * pick.shape[1] * D,
        moved=2 * rows * D,
    )(pick, chosen, *blocks)


def partial_kernel(pick_ref, back_ref, *out_refs):
    tokens, width = out_refs[0].shape
    for b, ref in enumerate(out_refs):
        pick = pick_ref[:, (b + 1) * tokens : (b + 2) * tokens]
        for c in range(0, width, WIDTH):
            at = slice(c, min(c + WIDTH, width))
            ref[:, at] = mm_tn(pick, back_ref[:, at]).astype(BF16)


def partials(pick, back, tokens):
    others = pick.shape[1] // tokens - 1
    rows, width = back.shape
    return call(
        partial_kernel,
        (jax.ShapeDtypeStruct((tokens, width), BF16),) * others,
        (1,),
        [whole(pick.shape), whole(back.shape)],
        (whole((tokens, width)),) * others,
        flops=2 * others * rows * width * tokens,
        moved=2 * rows * width,
    )(pick, back)


def state_kernel(k_ref, v_ref, out_ref):
    for h in range(HB):
        out_ref[h] = mm_tn(k_ref[:, head(h)], v_ref[:, head(h)]).astype(BF16)


def state_terms(k, v):
    tokens = k.shape[0]
    return call(
        state_kernel,
        jax.ShapeDtypeStruct((H, DH, DH), BF16),
        (H // HB,),
        [columns(tokens), columns(tokens)],
        per_head(),
        flops=2 * tokens * D * DH,
        moved=6 * tokens * D,
    )(k, v)


def running_kernel(backwards, states, in_ref, out_ref):
    n, rows, _ = in_ref.shape
    total = jnp.zeros((states, DH), F32)
    for i in reversed(range(n)) if backwards else range(n):
        out_ref[i, :states] = total.astype(BF16)
        total += in_ref[i, :states].astype(F32)
    if rows > states:
        half = (rows - states) // 2
        whole_sum = jnp.zeros((half, DH), F32)
        for i in range(n):
            whole_sum += in_ref[i, states : states + half].astype(F32)
            whole_sum += in_ref[i, states + half :].astype(F32)
        high, low = halves(whole_sum)
        for i in range(n):
            out_ref[i, states : states + half] = high
            out_ref[i, states + half :] = low


def to_heads(block):
    return lax.all_to_all(block, "ctx", split_axis=0, concat_axis=0, tiled=True)


def running_sum(here, backwards):
    states = H // here.shape[0] * DH
    return call(
        functools.partial(running_kernel, backwards, states),
        jax.ShapeDtypeStruct(here.shape, BF16),
        (1,),
        [whole(here.shape)],
        whole(here.shape),
        flops=here.size,
        moved=4 * here.size,
    )(here)


def forward_kernel(
    q_ref, k_ref, v_ref, prior_ref, earlier_ref, gain_ref, router_ref, ids_ref,
    z_ref, att_ref, sig_ref, logits_ref,
):
    tokens = q_ref.shape[0]
    causal = causal_mask(tokens)
    step = pl.program_id(0)

    @pl.when(step == 0)
    def _():
        logits_ref[...] = jnp.zeros_like(logits_ref)

    for h in range(HB):
        q, k, v = q_ref[:, head(h)], k_ref[:, head(h)], v_ref[:, head(h)]
        high, low = halves(prior_ref[h] + earlier_ref[h].astype(F32))
        scores = jnp.where(causal, mm_nt(q, k), 0.0).astype(BF16)
        att = mm(scores, v) + mm(q, high) + mm(q, low)
        mean = jnp.mean(att * att, axis=1, keepdims=True)
        z = (att / jnp.sqrt(mean + EPS) * gain_ref[:, head(h)]).astype(BF16)
        att_ref[:, head(h)] = att
        z_ref[:, head(h)] = z
    logits_ref[...] += mm(z_ref[...], router_ref[...])

    @pl.when(step == pl.num_programs(0) - 1)
    def _():
        experts = sig_ref.shape[1]
        lane = lax.broadcasted_iota(jnp.int32, (tokens, experts), 1)
        chosen = jnp.zeros((tokens, experts), F32)
        for j in range(ids_ref.shape[1]):
            chosen += (ids_ref[:, j : j + 1] == lane).astype(F32)
        sig_ref[...] = jax.nn.sigmoid(logits_ref[...]) * chosen


def attention_forward(q, k, v, prior, earlier, gain, router, ids):
    tokens, experts = q.shape[0], router.shape[1]
    return call(
        forward_kernel,
        (
            jax.ShapeDtypeStruct((tokens, D), BF16),
            jax.ShapeDtypeStruct((tokens, D), F32),
            jax.ShapeDtypeStruct((tokens, experts), F32),
        ),
        (H // HB,),
        [
            columns(tokens),
            columns(tokens),
            columns(tokens),
            per_head(),
            per_head(),
            columns(1),
            pl.BlockSpec((HEADS, experts), lambda i: (i, 0)),
            whole(ids.shape),
        ],
        (columns(tokens), columns(tokens), whole((tokens, experts))),
        scratch=[pltpu.VMEM((tokens, experts), F32)],
        flops=2 * tokens * D * 4 * DH,
        moved=2 * D * 8 * tokens,
    )(q, k, v, prior, earlier, gain, router, ids)


def router_kernel(*refs):
    z_ref, dg_ref, pick_ref, sig_ref, *more_refs, dlog_ref, term_ref = refs
    tokens, experts = sig_ref.shape

    @pl.when(pl.program_id(0) == 0)
    def _():
        sig = sig_ref[...]
        both = mm_tn(pick_ref[:, :tokens], dg_ref[...])
        for ref in more_refs:
            both += ref[...].astype(F32)
        dg = both[:, :experts] + both[:, experts : 2 * experts]
        total = jnp.sum(sig, axis=1, keepdims=True)
        mean = jnp.sum(sig * dg, axis=1, keepdims=True) / total
        dlog = sig * (1.0 - sig) * (dg - mean) / total
        for i, part in enumerate(thirds(dlog)):
            dlog_ref[i] = part

    z = z_ref[...]
    term_ref[...] = mm_tn(dlog_ref[0], z) + mm_tn(dlog_ref[1], z) + mm_tn(dlog_ref[2], z)


def router_gradient(z, back, more, pick, sig):
    tokens, experts = sig.shape
    rows = pick.shape[0]
    wide = lanes_of(2 * experts)
    return call(
        router_kernel,
        (
            jax.ShapeDtypeStruct((3, tokens, experts), BF16),
            jax.ShapeDtypeStruct((experts, D), F32),
        ),
        (D // WIDTH,),
        [
            columns(tokens, WIDTH),
            whole((rows, wide)),
            whole(pick.shape),
            whole(sig.shape),
        ]
        + [whole((tokens, wide))] * len(more),
        (whole((3, tokens, experts)), columns(experts, WIDTH)),
        flops=6 * tokens * experts * D,
        moved=2 * tokens * D,
    )(z, back, pick, sig, *more)


def middle_kernel(*refs):
    q_ref, att_ref, dy_ref, back_ref, pick_ref, dlog_ref, gain_ref, router_ref, rterm_ref = refs[:9]
    *more_refs, datt_ref, term_ref = refs[9:]
    experts = router_ref.shape[1]
    per = HB // term_ref.shape[0]
    tokens = q_ref.shape[0]
    router = router_ref[...]
    dz = dy_ref[...].astype(F32) + mm_tn(pick_ref[:, :tokens], back_ref[...])
    for ref in more_refs:
        dz += ref[...].astype(F32)
    for i in range(3):
        dz += mm_nt(dlog_ref[i], router)
    weighted = dz * gain_ref[...]
    for h in range(HB):
        att, w = att_ref[:, head(h)], weighted[:, head(h)]
        mean = jnp.mean(att * att, axis=1, keepdims=True) + EPS
        inner = jnp.sum(w * att, axis=1, keepdims=True)
        datt = ((w - att * (inner / (DH * mean))) / jnp.sqrt(mean)).astype(BF16)
        datt_ref[:, head(h)] = datt
        to, i = h // per, h % per
        term_ref[to, head(i)] = mm_tn(q_ref[:, head(h)], datt).astype(BF16)
        high, low = halves(rterm_ref[:, head(h)])
        at = per * DH + i * experts
        term_ref[to, at : at + experts] = high
        term_ref[to, at + per * experts : at + per * experts + experts] = low


def attention_middle(q, att, dy, back, more, pick, dlog, gain, router, rterm, n):
    tokens, rows, experts = q.shape[0], pick.shape[0], router.shape[1]
    per = H // n
    length = per * (DH + 2 * experts)
    return call(
        middle_kernel,
        (
            jax.ShapeDtypeStruct((tokens, D), BF16),
            jax.ShapeDtypeStruct((n, length, DH), BF16),
        ),
        (H // HB,),
        [
            columns(tokens),
            columns(tokens),
            columns(tokens),
            columns(rows),
            whole(pick.shape),
            whole(dlog.shape),
            columns(1),
            pl.BlockSpec((HEADS, experts), lambda i: (i, 0)),
            columns(experts),
        ]
        + [columns(tokens)] * len(more),
        (columns(tokens), pl.BlockSpec((HB // per, length, DH), lambda i: (i, 0, 0))),
        flops=2 * tokens * D * (DH + rows + 3 * experts),
        moved=2 * D * (8 * tokens + rows),
    )(q, att, dy, back, pick, dlog, gain, router, rterm, *more)


def early_kernel(q_ref, k_ref, v_ref, datt_ref, prior_ref, earlier_ref, gq_ref, gk_ref, gv_ref):
    causal = causal_mask(q_ref.shape[0])
    for h in range(HB):
        q, k, v = q_ref[:, head(h)], k_ref[:, head(h)], v_ref[:, head(h)]
        datt = datt_ref[:, head(h)]
        high, low = halves(prior_ref[h] + earlier_ref[h].astype(F32))
        dscores = jnp.where(causal, mm_nt(datt, v), 0.0).astype(BF16)
        scores = jnp.where(causal, mm_nt(q, k), 0.0).astype(BF16)
        gq = mm(dscores, k) + mm_nt(datt, high) + mm_nt(datt, low)
        gq_ref[:, head(h)] = gq.astype(BF16)
        gk_ref[:, head(h)] = mm_tn(dscores, q)
        gv_ref[:, head(h)] = mm_tn(scores, datt)


def attention_early(q, k, v, datt, prior, earlier):
    tokens = q.shape[0]
    block = columns(tokens)
    return call(
        early_kernel,
        (
            jax.ShapeDtypeStruct((tokens, D), BF16),
            jax.ShapeDtypeStruct((tokens, D), F32),
            jax.ShapeDtypeStruct((tokens, D), F32),
        ),
        (H // HB,),
        [block, block, block, block, per_head(), per_head()],
        (block, block, block),
        flops=2 * tokens * D * DH * 7,
        moved=22 * D * tokens,
    )(q, k, v, datt, prior, earlier)


def late_kernel(k_ref, v_ref, later_ref, gk_ref, gv_ref, out_k_ref, out_v_ref, router_ref):
    experts = router_ref.shape[0]
    per = HB // later_ref.shape[0]
    for h in range(HB):
        to, i = h // per, h % per
        later = later_ref[to, head(i)]
        out_k_ref[:, head(h)] = (gk_ref[:, head(h)] + mm_nt(v_ref[:, head(h)], later)).astype(BF16)
        out_v_ref[:, head(h)] = (gv_ref[:, head(h)] + mm(k_ref[:, head(h)], later)).astype(BF16)
        at = per * DH + i * experts
        high = later_ref[to, at : at + experts].astype(F32)
        low = later_ref[to, at + per * experts : at + per * experts + experts].astype(F32)
        router_ref[:, head(h)] = high + low


def attention_late(k, v, later, gk, gv, experts):
    tokens = k.shape[0]
    block = columns(tokens)
    out = jax.ShapeDtypeStruct((tokens, D), BF16)
    n, length, _ = later.shape
    return call(
        late_kernel,
        (out, out, jax.ShapeDtypeStruct((experts, D), F32)),
        (H // HB,),
        [
            block,
            block,
            pl.BlockSpec((HB * n // H, length, DH), lambda i: (i, 0, 0)),
            block,
            block,
        ],
        (block, block, columns(experts)),
        flops=2 * tokens * D * DH * 2,
        moved=18 * D * tokens,
    )(k, v, later, gk, gv)


def output_kernel(z_ref, pick_ref, back_ref, *refs):
    *more_refs, out_ref = refs
    tokens = z_ref.shape[0]
    total = z_ref[...].astype(F32) + mm_tn(pick_ref[:, :tokens], back_ref[...])
    for ref in more_refs:
        total += ref[...].astype(F32)
    out_ref[...] = total.astype(BF16)


def layer_output(z, pick, back, more):
    tokens, rows = z.shape[0], pick.shape[0]
    return call(
        output_kernel,
        jax.ShapeDtypeStruct((tokens, D), BF16),
        (D // HEADS,),
        [columns(tokens), whole(pick.shape), columns(rows)] + [columns(tokens)] * len(more),
        columns(tokens),
        flops=2 * tokens * D * rows,
        moved=2 * D * rows,
    )(z, pick, back, *more)


def down_kernel(dy_ref, down_ref, out_ref):
    out_ref[...] = mm_nt(dy_ref[...], down_ref[...])


def expert_down_back(dy_rows, down_mat):
    rows, hidden = dy_rows.shape[0], down_mat.shape[0]
    tile = 256
    return call(
        down_kernel,
        jax.ShapeDtypeStruct((rows, hidden), F32),
        (hidden // tile,),
        [
            pl.BlockSpec((rows, D), lambda i: (0, 0)),
            pl.BlockSpec((tile, D), lambda i: (i, 0)),
        ],
        columns(rows, tile),
        flops=2 * rows * hidden * D,
        moved=2 * (rows + hidden) * D,
    )(dy_rows, down_mat)


def expert_kernel(
    me_ref, z_ref, mask_ref, router_ref, gate_ref, up_ref, dh_ref,
    hid_ref, dgp_ref, dup_ref, weight_ref, pair_ref, dg_ref,
):
    experts = router_ref.shape[1]

    @pl.when(pl.program_id(0) == 0)
    def _():
        sig = jax.nn.sigmoid(mm(z_ref[...], router_ref[...]))
        sig *= mask_ref[:, :experts].astype(F32)
        total = jnp.sum(sig, axis=1, keepdims=True)
        lane = lax.broadcasted_iota(jnp.int32, sig.shape, 1)
        mine = jnp.sum(jnp.where(lane == me_ref[0, 0], sig, 0.0), axis=1, keepdims=True)
        some = total > 0
        weight_ref[...] = jnp.where(some, mine / jnp.where(some, total, 1.0), 0.0)
        dg_ref[...] = jnp.zeros_like(dg_ref)

    z = z_ref[...]
    gp = mm(z, gate_ref[...])
    up = mm(z, up_ref[...])
    gs = jax.nn.sigmoid(gp)
    hid = (gp * gs * up).astype(BF16)
    plain = dh_ref[...]
    dg_ref[...] += jnp.sum(plain * hid.astype(F32), axis=1, keepdims=True)
    dh = plain * weight_ref[...]
    hid_ref[...] = hid
    dgp_ref[...] = (dh * up * gs * (1.0 + gp * (1.0 - gs))).astype(BF16)
    dup_ref[...] = (dh * gp * gs).astype(BF16)

    @pl.when(pl.program_id(0) == pl.num_programs(0) - 1)
    def _():
        lane = lax.broadcasted_iota(jnp.int32, pair_ref.shape, 1)
        dg = dg_ref[...]
        high = dg.astype(BF16).astype(F32)
        pair = jnp.where(lane == me_ref[0, 0], high, 0.0)
        pair = jnp.where(lane == me_ref[0, 0] + experts, dg - high, pair)
        pair_ref[...] = pair.astype(BF16)


def expert_forward(me, z_rows, dy_rows, router, gate_mat, up_mat, dh_plain):
    rows, hidden, experts = z_rows.shape[0], gate_mat.shape[1], router.shape[1]
    tile, wide = 256, lanes_of(experts)
    beside = D // wide
    inner = jax.ShapeDtypeStruct((rows, hidden), BF16)
    column = jax.ShapeDtypeStruct((rows, 1), F32)
    pair = jax.ShapeDtypeStruct((rows, lanes_of(2 * experts)), BF16)
    return call(
        expert_kernel,
        (inner, inner, inner, column, pair),
        (hidden // tile,),
        [
            smem(),
            whole((rows, D)),
            pl.BlockSpec((rows, wide), lambda i: (0, beside)),
            whole(router.shape),
            columns(D, tile),
            columns(D, tile),
            columns(rows, tile),
        ],
        (columns(rows, tile),) * 3 + (whole((rows, 1)), whole(pair.shape)),
        scratch=[pltpu.VMEM((rows, 1), F32)],
        flops=4 * rows * hidden * D,
        moved=2 * (rows + 2 * hidden) * D,
    )(me, z_rows, dy_rows, router, gate_mat, up_mat, dh_plain)


def back_kernel(dgp_ref, dup_ref, gate_ref, up_ref, weight_ref, out_ref):
    total = mm_nt(dgp_ref[...], gate_ref[...]) + mm_nt(dup_ref[...], up_ref[...])
    out_ref[...] = (total * weight_ref[...]).astype(BF16)


def expert_back(dgp, dup, gate_mat, up_mat, weight):
    rows, hidden = dgp.shape
    stripe = pl.BlockSpec((WIDTH, hidden), lambda i: (i, 0))
    return call(
        back_kernel,
        jax.ShapeDtypeStruct((rows, D), BF16),
        (D // WIDTH,),
        [whole(dgp.shape), whole(dup.shape), stripe, stripe, whole((rows, 1))],
        columns(rows, WIDTH),
        flops=4 * rows * hidden * D,
        moved=2 * (rows + 2 * hidden) * D,
    )(dgp, dup, gate_mat, up_mat, weight)


def product_kernel(hid_ref, down_ref, weight_ref, out_ref):
    out_ref[...] = (mm(hid_ref[...], down_ref[...]) * weight_ref[...]).astype(BF16)


def expert_product(hid, down_mat, weight):
    rows, hidden = hid.shape
    return call(
        product_kernel,
        jax.ShapeDtypeStruct((rows, D), BF16),
        (D // WIDTH,),
        [whole(hid.shape), columns(hidden, WIDTH), whole((rows, 1))],
        columns(rows, WIDTH),
        flops=2 * rows * hidden * D,
        moved=2 * (rows + hidden) * D,
    )(hid, down_mat, weight)


def weights_kernel(
    z_ref, dy_ref, hid_ref, dgp_ref, dup_ref, weight_ref, gate_ref, up_ref, down_ref
):
    z = z_ref[...]
    gate_ref[...] = mm_tn(z, dgp_ref[...]).astype(BF16)
    up_ref[...] = mm_tn(z, dup_ref[...]).astype(BF16)
    de = (dy_ref[...].astype(F32) * weight_ref[...]).astype(BF16)
    down_ref[...] = mm_tn(hid_ref[...], de).astype(BF16)


def expert_weights(z_rows, dy_rows, hid, dgp, dup, weight):
    rows, hidden = hid.shape
    stripe = pl.BlockSpec((WIDTH, hidden), lambda i: (i, 0))
    return call(
        weights_kernel,
        (
            jax.ShapeDtypeStruct((D, hidden), BF16),
            jax.ShapeDtypeStruct((D, hidden), BF16),
            jax.ShapeDtypeStruct((hidden, D), BF16),
        ),
        (D // WIDTH,),
        [columns(rows, WIDTH), columns(rows, WIDTH)] + [whole(hid.shape)] * 3 + [whole((rows, 1))],
        (stripe, stripe, columns(hidden, WIDTH)),
        flops=6 * rows * hidden * D,
        moved=2 * (2 * rows + 3 * hidden) * D,
    )(z_rows, dy_rows, hid, dgp, dup, weight)


def exchange(rows):
    group = lax.axis_size("ctx")
    shaped = rows.reshape(group, rows.shape[0] // group, rows.shape[1])
    moved = lax.all_to_all(shaped, "ctx", split_axis=0, concat_axis=0, tiled=True)
    return moved.reshape(rows.shape)


def after(value, *earlier):
    return lax.optimization_barrier((value, *earlier))[0]


def swap(block, axis, by=1):
    return lax.ppermute(block, axis, [(i, i ^ by) for i in range(lax.axis_size(axis))])


def peers():
    return [(b % 2, b // 2) for b in range(2 * lax.axis_size("near"))]


def replicate(block, *gate):
    far = swap(block, "far")
    near = range(1, lax.axis_size("near"))
    own = [swap(block, "near", n) for n in near]
    gated = after(far, *gate) if gate else far
    other = [swap(gated, "near", n) for n in near]
    return [block, far] + [x for pair in zip(own, other) for x in pair]


def collect_far(parts):
    far = parts[0]
    near = range(1, lax.axis_size("near"))
    if len(near):
        arrived = [swap(parts[2 * n], "near", n) for n in near]
        far = sum((a.astype(F32) for a in arrived), far.astype(F32)).astype(BF16)
    return far


def collect(parts, far):
    near = range(1, lax.axis_size("near"))
    return [swap(far, "far")] + [swap(parts[2 * n - 1], "near", n) for n in near]


def collect_small(parts):
    near = lax.axis_size("near")
    steps = peers()[1:]
    return [swap(part, ("far", "near"), f * near + n) for part, (f, n) in zip(parts, steps)]


def doublings():
    steps = []
    for axis in ("far", "near"):
        by = 1
        while by < lax.axis_size(axis):
            steps.append((axis, by))
            by *= 2
    return steps


def sum_over(term, steps, gate):
    for axis, by in steps:
        term = term + after(swap(term, axis, by), gate)
    return term


def local(
    queries,
    keys,
    values,
    prior_state,
    norm_gain,
    router_weight,
    expert_ids,
    w_gate,
    w_up,
    w_down,
    cotangent,
):
    q, k, v, dy = queries[0], keys[0], values[0], cotangent[0]
    tokens = q.shape[0]
    experts = router_weight.shape[1]
    cap = max(2, 3 * tokens * TOPK // (2 * experts))
    gate_mat, up_mat, down_mat = w_gate[0], w_up[0], w_down[0]
    prior = prior_state[0]
    gain = norm_gain.reshape(1, D)
    me = jnp.stack([lax.axis_index(ALL), jnp.int32(experts)]).reshape(1, 2).astype(jnp.int32)
    plane = lax.axis_index(("far", "near")).reshape(1, 1).astype(jnp.int32)
    rows = experts * cap

    n = lax.axis_size("ctx")
    ids = expert_ids[0]
    beside = jnp.pad(ids.astype(BF16), ((0, 0), (0, 128 - TOPK)))
    terms = state_terms(k, v).reshape(n, H // n * DH, DH)
    here = to_heads(terms)
    sums = running_sum(here, False)
    dy_blocks = replicate(jnp.concatenate([dy, beside], axis=1), sums)
    earlier = to_heads(sums).reshape(H, DH, DH)
    z, att, sig = attention_forward(q, k, v, prior, earlier, gain, router_weight, ids)
    z_blocks = replicate(z)
    pick, chosen = route(plane, after(dy_blocks, z), experts, rows, cap)
    dy_rows = exchange(gather(pick, chosen, dy_blocks, True))
    z_rows = exchange(gather(pick, chosen, z_blocks, False))

    dh_plain = expert_down_back(dy_rows, down_mat)
    hid, dgp, dup, weight, dg_send = expert_forward(
        me, z_rows, dy_rows, router_weight, gate_mat, up_mat, dh_plain
    )
    dg_back = exchange(dg_send)
    dz_send = expert_back(dgp, dup, gate_mat, up_mat, weight)
    dz_back = exchange(dz_send)
    dg_more = collect_small(partials(pick, after(dg_back, dz_send), tokens))
    dlog, rterm = router_gradient(z, dg_back, dg_more, pick, sig)
    eo_send = expert_product(after(hid, dlog), down_mat, weight)
    steps = doublings()
    rterm = sum_over(rterm, steps[:1], eo_send)
    grad_gate, grad_up, grad_down = expert_weights(
        after(z_rows, rterm), dy_rows, hid, dgp, dup, weight
    )
    rterm = sum_over(rterm, steps[1:], grad_gate)

    dz_parts = partials(pick, after(dz_back, rterm), tokens)
    dz_far = collect_far(dz_parts)
    dz_more = collect(dz_parts, dz_far)
    eo_back = exchange(after(eo_send, *dz_parts))
    datt, dterms = attention_middle(
        q, att, dy, dz_back, dz_more, pick, dlog, gain, router_weight, rterm, n
    )
    there = to_heads(dterms)
    eo_parts = partials(pick, after(eo_back, datt), tokens)
    eo_more = collect(eo_parts, collect_far(eo_parts))
    gq, gk, gv = attention_early(q, k, v, after(datt, *eo_parts), prior, earlier)
    later = to_heads(running_sum(there, True))
    grad_k, grad_v, grad_router = attention_late(k, v, later, gk, gv, experts)
    grad_router = grad_router.T
    output = layer_output(z, pick, eo_back, eo_more)
    return (
        output[None],
        gq[None],
        grad_k[None],
        grad_v[None],
        grad_gate[None],
        grad_up[None],
        grad_down[None],
        grad_router,
    )


def solution(mesh):
    tokens = P(("far", "near"), "ctx", None)
    weights = P(ALL, None, None)
    split = Mesh(
        mesh.devices.reshape(2, mesh.shape["dp"] // 2, mesh.shape["ctx"]), ("far", "near", "ctx")
    )
    placed = (
        tokens,
        tokens,
        tokens,
        P(("far", "near"), None, None, None),
        P(),
        P(),
        tokens,
        weights,
        weights,
        weights,
        tokens,
    )
    return jax.shard_map(
        local,
        mesh=split,
        in_specs=placed,
        out_specs=(tokens, tokens, tokens, tokens, weights, weights, weights, P()),
        check_vma=False,
    )
```

```python
import functools

import jax
import jax.numpy as jnp
from jax import lax
from jax.experimental import pallas as pl
from jax.experimental.pallas import tpu as pltpu
from jax.sharding import Mesh
from jax.sharding import PartitionSpec as P

H = 16
DH = 128
D = 2048
TOPK = 4
HB = 8
WIDTH = 512
HEADS = HB * DH
EPS = 1e-05
ALL = ("far", "near", "ctx")
F32 = jnp.float32
BF16 = jnp.bfloat16
LIMIT = 62 << 20


def mm(a, b):
    return jnp.dot(a, b, preferred_element_type=F32)


def mm_tn(a, b):
    return lax.dot_general(a, b, (((0,), (0,)), ((), ())), preferred_element_type=F32)


def mm_nt(a, b):
    return lax.dot_general(a, b, (((1,), (1,)), ((), ())), preferred_element_type=F32)


def halves(x):
    high = x.astype(BF16)
    return high, (x - high.astype(F32)).astype(BF16)


def thirds(x):
    high, rest = x.astype(BF16), None
    rest = x - high.astype(F32)
    middle = rest.astype(BF16)
    return high, middle, (rest - middle.astype(F32)).astype(BF16)


def causal_mask(n):
    return lax.broadcasted_iota(jnp.int32, (n, n), 0) >= lax.broadcasted_iota(jnp.int32, (n, n), 1)


def head(h):
    return slice(h * DH, (h + 1) * DH)


def call(kernel, out_shape, grid, in_specs, out_specs, scratch=(), flops=0, moved=0):
    return pl.pallas_call(
        kernel,
        out_shape=out_shape,
        grid=grid,
        in_specs=in_specs,
        out_specs=out_specs,
        scratch_shapes=scratch,
        compiler_params=pltpu.CompilerParams(vmem_limit_bytes=LIMIT),
        cost_estimate=pl.CostEstimate(flops=flops, bytes_accessed=moved, transcendentals=0),
    )


def whole(shape):
    return pl.BlockSpec(shape, lambda *_: (0,) * len(shape))


def columns(rows, width=HEADS):
    return pl.BlockSpec((rows, width), lambda i: (0, i))


def per_head(n=HB):
    return pl.BlockSpec((n, DH, DH), lambda i: (i, 0, 0))


def lanes_of(n):
    return -(-n // 128) * 128


def route_kernel(cap, top, plane_ref, *refs):
    *ids_refs, pick_ref, chosen_ref = refs
    tokens = ids_refs[0].shape[0]
    experts = chosen_ref.shape[1]
    rows = pick_ref.shape[0]
    slots = len(ids_refs) * cap
    group = rows // slots
    row = lax.broadcasted_iota(jnp.int32, (rows, experts), 0)
    first = lax.broadcasted_iota(jnp.int32, (rows, experts), 1) - plane_ref[0, 0] * group
    first = first * slots
    owns = (row >= first) & (row < first + slots)
    wanted = jnp.sum(jnp.where(owns, row - first + 1, 0), axis=1, keepdims=True).astype(F32)
    owns = owns.astype(F32).astype(BF16)
    lane = lax.broadcasted_iota(jnp.int32, (tokens, experts), 1)
    earlier = causal_mask(tokens).astype(F32).astype(BF16)
    for b, ref in enumerate(ids_refs):
        ids = ref[...].astype(F32)
        chosen = jnp.zeros((tokens, experts), F32)
        for j in range(top):
            chosen += (ids[:, j : j + 1] == lane.astype(F32)).astype(F32)
        place = chosen * (mm(earlier, chosen.astype(BF16)) + float(b * cap))
        found = mm_nt(owns, place.astype(BF16))
        at = slice(b * tokens, (b + 1) * tokens)
        pick_ref[:, at] = (found == wanted).astype(F32).astype(BF16)
        chosen_ref[at] = chosen


def smem():
    return pl.BlockSpec(memory_space=pltpu.SMEM)


def gather_kernel(masked, pick_ref, chosen_ref, *refs):
    *block_refs, send_ref, stack_ref = refs
    tokens = block_refs[0].shape[0]
    pick = pick_ref[...]
    for b, ref in enumerate(block_refs):
        stack_ref[b * tokens : (b + 1) * tokens] = ref[:, :D]
    for c in range(D // WIDTH):
        at = slice(c * WIDTH, (c + 1) * WIDTH)
        send_ref[:, at] = mm(pick, stack_ref[:, at]).astype(BF16)
    if masked:
        experts = chosen_ref.shape[1]
        if send_ref.shape[1] > D + experts:
            send_ref[:, D:] = jnp.zeros((send_ref.shape[0], send_ref.shape[1] - D), BF16)
        mask = mm(pick, chosen_ref[...].astype(BF16))
        send_ref[:, D : D + experts] = mask.astype(BF16)


def gather(pick, chosen, blocks, masked):
    rows = pick.shape[0]
    width = D + (lanes_of(chosen.shape[1]) if masked else 0)
    return call(
        functools.partial(gather_kernel, masked),
        jax.ShapeDtypeStruct((rows, width), BF16),
        (1,),
        [whole(pick.shape), whole(chosen.shape)] + [whole(blocks[0].shape)] * len(blocks),
        whole((rows, width)),
        scratch=[pltpu.VMEM((pick.shape[1], D), BF16)],
        flops=2 * rows * pick.shape[1] * D,
        moved=2 * rows * D,
    )(pick, chosen, *blocks)


def route_gather_kernel(cap, top, plane_ref, *refs):
    *block_refs, pick_ref, chosen_ref, send_ref, stack_ref = refs
    ids_refs = [ref.at[:, D : D + 128] for ref in block_refs]
    route_kernel(cap, top, plane_ref, *ids_refs, pick_ref, chosen_ref)
    gather_kernel(True, pick_ref, chosen_ref, *block_refs, send_ref, stack_ref)


def route_gather(plane, blocks, experts, rows, cap):
    tokens, n = blocks[0].shape[0], len(blocks)
    width = D + lanes_of(experts)
    return call(
        functools.partial(route_gather_kernel, cap, TOPK),
        (
            jax.ShapeDtypeStruct((rows, n * tokens), BF16),
            jax.ShapeDtypeStruct((n * tokens, experts), F32),
            jax.ShapeDtypeStruct((rows, width), BF16),
        ),
        (1,),
        [smem()] + [whole(blocks[0].shape)] * n,
        (whole((rows, n * tokens)), whole((n * tokens, experts)), whole((rows, width))),
        scratch=[pltpu.VMEM((n * tokens, D), BF16)],
        flops=2 * n * rows * tokens * D,
        moved=2 * rows * D,
    )(plane, *blocks)


def partial_kernel(pick_ref, back_ref, *out_refs):
    tokens, width = out_refs[0].shape
    for b, ref in enumerate(out_refs):
        pick = pick_ref[:, (b + 1) * tokens : (b + 2) * tokens]
        for c in range(0, width, WIDTH):
            at = slice(c, min(c + WIDTH, width))
            ref[:, at] = mm_tn(pick, back_ref[:, at]).astype(BF16)


def partials(pick, back, tokens):
    others = pick.shape[1] // tokens - 1
    rows, width = back.shape
    return call(
        partial_kernel,
        (jax.ShapeDtypeStruct((tokens, width), BF16),) * others,
        (1,),
        [whole(pick.shape), whole(back.shape)],
        (whole((tokens, width)),) * others,
        flops=2 * others * rows * width * tokens,
        moved=2 * rows * width,
    )(pick, back)


def state_kernel(k_ref, v_ref, out_ref):
    for h in range(HB):
        out_ref[h] = mm_tn(k_ref[:, head(h)], v_ref[:, head(h)]).astype(BF16)


def state_terms(k, v):
    tokens = k.shape[0]
    return call(
        state_kernel,
        jax.ShapeDtypeStruct((H, DH, DH), BF16),
        (H // HB,),
        [columns(tokens), columns(tokens)],
        per_head(),
        flops=2 * tokens * D * DH,
        moved=6 * tokens * D,
    )(k, v)


def running_kernel(backwards, states, in_ref, out_ref):
    n, rows, _ = in_ref.shape
    total = jnp.zeros((states, DH), F32)
    for i in reversed(range(n)) if backwards else range(n):
        out_ref[i, :states] = total.astype(BF16)
        total += in_ref[i, :states].astype(F32)
    if rows > states:
        half = (rows - states) // 2
        whole_sum = jnp.zeros((half, DH), F32)
        for i in range(n):
            whole_sum += in_ref[i, states : states + half].astype(F32)
            whole_sum += in_ref[i, states + half :].astype(F32)
        high, low = halves(whole_sum)
        for i in range(n):
            out_ref[i, states : states + half] = high
            out_ref[i, states + half :] = low


def to_heads(block):
    return lax.all_to_all(block, "ctx", split_axis=0, concat_axis=0, tiled=True)


def running_sum(here, backwards):
    states = H // here.shape[0] * DH
    return call(
        functools.partial(running_kernel, backwards, states),
        jax.ShapeDtypeStruct(here.shape, BF16),
        (1,),
        [whole(here.shape)],
        whole(here.shape),
        flops=here.size,
        moved=4 * here.size,
    )(here)


def forward_kernel(
    q_ref, k_ref, v_ref, prior_ref, earlier_ref, gain_ref, router_ref, ids_ref,
    z_ref, att_ref, sig_ref, logits_ref,
):
    tokens = q_ref.shape[0]
    causal = causal_mask(tokens)
    step = pl.program_id(0)

    @pl.when(step == 0)
    def _():
        logits_ref[...] = jnp.zeros_like(logits_ref)

    for h in range(HB):
        q, k, v = q_ref[:, head(h)], k_ref[:, head(h)], v_ref[:, head(h)]
        high, low = halves(prior_ref[h] + earlier_ref[h].astype(F32))
        scores = jnp.where(causal, mm_nt(q, k), 0.0).astype(BF16)
        att = mm(scores, v) + mm(q, high) + mm(q, low)
        mean = jnp.mean(att * att, axis=1, keepdims=True)
        z = (att / jnp.sqrt(mean + EPS) * gain_ref[:, head(h)]).astype(BF16)
        att_ref[:, head(h)] = att
        z_ref[:, head(h)] = z
    logits_ref[...] += mm(z_ref[...], router_ref[...])

    @pl.when(step == pl.num_programs(0) - 1)
    def _():
        experts = sig_ref.shape[1]
        lane = lax.broadcasted_iota(jnp.int32, (tokens, experts), 1)
        chosen = jnp.zeros((tokens, experts), F32)
        for j in range(ids_ref.shape[1]):
            chosen += (ids_ref[:, j : j + 1] == lane).astype(F32)
        sig_ref[...] = jax.nn.sigmoid(logits_ref[...]) * chosen


def attention_forward(q, k, v, prior, earlier, gain, router, ids):
    tokens, experts = q.shape[0], router.shape[1]
    return call(
        forward_kernel,
        (
            jax.ShapeDtypeStruct((tokens, D), BF16),
            jax.ShapeDtypeStruct((tokens, D), F32),
            jax.ShapeDtypeStruct((tokens, experts), F32),
        ),
        (H // HB,),
        [
            columns(tokens),
            columns(tokens),
            columns(tokens),
            per_head(),
            per_head(),
            columns(1),
            pl.BlockSpec((HEADS, experts), lambda i: (i, 0)),
            whole(ids.shape),
        ],
        (columns(tokens), columns(tokens), whole((tokens, experts))),
        scratch=[pltpu.VMEM((tokens, experts), F32)],
        flops=2 * tokens * D * 4 * DH,
        moved=2 * D * 8 * tokens,
    )(q, k, v, prior, earlier, gain, router, ids)


def router_kernel(*refs):
    z_ref, dg_ref, pick_ref, sig_ref, *more_refs, dlog_ref, term_ref = refs
    tokens, experts = sig_ref.shape

    @pl.when(pl.program_id(0) == 0)
    def _():
        sig = sig_ref[...]
        both = mm_tn(pick_ref[:, :tokens], dg_ref[...])
        for ref in more_refs:
            both += ref[...].astype(F32)
        dg = both[:, :experts] + both[:, experts : 2 * experts]
        total = jnp.sum(sig, axis=1, keepdims=True)
        mean = jnp.sum(sig * dg, axis=1, keepdims=True) / total
        dlog = sig * (1.0 - sig) * (dg - mean) / total
        for i, part in enumerate(thirds(dlog)):
            dlog_ref[i] = part

    z = z_ref[...]
    term_ref[...] = mm_tn(dlog_ref[0], z) + mm_tn(dlog_ref[1], z) + mm_tn(dlog_ref[2], z)


def router_gradient(z, back, more, pick, sig):
    tokens, experts = sig.shape
    rows = pick.shape[0]
    wide = lanes_of(2 * experts)
    return call(
        router_kernel,
        (
            jax.ShapeDtypeStruct((3, tokens, experts), BF16),
            jax.ShapeDtypeStruct((experts, D), F32),
        ),
        (D // WIDTH,),
        [
            columns(tokens, WIDTH),
            whole((rows, wide)),
            whole(pick.shape),
            whole(sig.shape),
        ]
        + [whole((tokens, wide))] * len(more),
        (whole((3, tokens, experts)), columns(experts, WIDTH)),
        flops=6 * tokens * experts * D,
        moved=2 * tokens * D,
    )(z, back, pick, sig, *more)


def middle_kernel(*refs):
    q_ref, att_ref, dy_ref, back_ref, pick_ref, dlog_ref, gain_ref, router_ref, rterm_ref = refs[:9]
    *more_refs, datt_ref, term_ref = refs[9:]
    experts = router_ref.shape[1]
    per = HB // term_ref.shape[0]
    tokens = q_ref.shape[0]
    router = router_ref[...]
    dz = dy_ref[...].astype(F32) + mm_tn(pick_ref[:, :tokens], back_ref[...])
    for ref in more_refs:
        dz += ref[...].astype(F32)
    for i in range(3):
        dz += mm_nt(dlog_ref[i], router)
    weighted = dz * gain_ref[...]
    for h in range(HB):
        att, w = att_ref[:, head(h)], weighted[:, head(h)]
        mean = jnp.mean(att * att, axis=1, keepdims=True) + EPS
        inner = jnp.sum(w * att, axis=1, keepdims=True)
        datt = ((w - att * (inner / (DH * mean))) / jnp.sqrt(mean)).astype(BF16)
        datt_ref[:, head(h)] = datt
        to, i = h // per, h % per
        term_ref[to, head(i)] = mm_tn(q_ref[:, head(h)], datt).astype(BF16)
        high, low = halves(rterm_ref[:, head(h)])
        at = per * DH + i * experts
        term_ref[to, at : at + experts] = high
        term_ref[to, at + per * experts : at + per * experts + experts] = low


def attention_middle(q, att, dy, back, more, pick, dlog, gain, router, rterm, n):
    tokens, rows, experts = q.shape[0], pick.shape[0], router.shape[1]
    per = H // n
    length = per * (DH + 2 * experts)
    return call(
        middle_kernel,
        (
            jax.ShapeDtypeStruct((tokens, D), BF16),
            jax.ShapeDtypeStruct((n, length, DH), BF16),
        ),
        (H // HB,),
        [
            columns(tokens),
            columns(tokens),
            columns(tokens),
            columns(rows),
            whole(pick.shape),
            whole(dlog.shape),
            columns(1),
            pl.BlockSpec((HEADS, experts), lambda i: (i, 0)),
            columns(experts),
        ]
        + [columns(tokens)] * len(more),
        (columns(tokens), pl.BlockSpec((HB // per, length, DH), lambda i: (i, 0, 0))),
        flops=2 * tokens * D * (DH + rows + 3 * experts),
        moved=2 * D * (8 * tokens + rows),
    )(q, att, dy, back, pick, dlog, gain, router, rterm, *more)


def early_kernel(q_ref, k_ref, v_ref, datt_ref, prior_ref, earlier_ref, gq_ref, gk_ref, gv_ref):
    causal = causal_mask(q_ref.shape[0])
    for h in range(HB):
        q, k, v = q_ref[:, head(h)], k_ref[:, head(h)], v_ref[:, head(h)]
        datt = datt_ref[:, head(h)]
        high, low = halves(prior_ref[h] + earlier_ref[h].astype(F32))
        dscores = jnp.where(causal, mm_nt(datt, v), 0.0).astype(BF16)
        scores = jnp.where(causal, mm_nt(q, k), 0.0).astype(BF16)
        gq = mm(dscores, k) + mm_nt(datt, high) + mm_nt(datt, low)
        gq_ref[:, head(h)] = gq.astype(BF16)
        gk_ref[:, head(h)] = mm_tn(dscores, q)
        gv_ref[:, head(h)] = mm_tn(scores, datt)


def attention_early(q, k, v, datt, prior, earlier):
    tokens = q.shape[0]
    block = columns(tokens)
    return call(
        early_kernel,
        (
            jax.ShapeDtypeStruct((tokens, D), BF16),
            jax.ShapeDtypeStruct((tokens, D), F32),
            jax.ShapeDtypeStruct((tokens, D), F32),
        ),
        (H // HB,),
        [block, block, block, block, per_head(), per_head()],
        (block, block, block),
        flops=2 * tokens * D * DH * 7,
        moved=22 * D * tokens,
    )(q, k, v, datt, prior, earlier)


def late_kernel(k_ref, v_ref, later_ref, gk_ref, gv_ref, out_k_ref, out_v_ref, router_ref):
    experts = router_ref.shape[0]
    per = HB // later_ref.shape[0]
    for h in range(HB):
        to, i = h // per, h % per
        later = later_ref[to, head(i)]
        out_k_ref[:, head(h)] = (gk_ref[:, head(h)] + mm_nt(v_ref[:, head(h)], later)).astype(BF16)
        out_v_ref[:, head(h)] = (gv_ref[:, head(h)] + mm(k_ref[:, head(h)], later)).astype(BF16)
        at = per * DH + i * experts
        high = later_ref[to, at : at + experts].astype(F32)
        low = later_ref[to, at + per * experts : at + per * experts + experts].astype(F32)
        router_ref[:, head(h)] = high + low


def attention_late(k, v, later, gk, gv, experts):
    tokens = k.shape[0]
    block = columns(tokens)
    out = jax.ShapeDtypeStruct((tokens, D), BF16)
    n, length, _ = later.shape
    return call(
        late_kernel,
        (out, out, jax.ShapeDtypeStruct((experts, D), F32)),
        (H // HB,),
        [
            block,
            block,
            pl.BlockSpec((HB * n // H, length, DH), lambda i: (i, 0, 0)),
            block,
            block,
        ],
        (block, block, columns(experts)),
        flops=2 * tokens * D * DH * 2,
        moved=18 * D * tokens,
    )(k, v, later, gk, gv)


def output_kernel(z_ref, pick_ref, back_ref, *refs):
    *more_refs, out_ref = refs
    tokens = z_ref.shape[0]
    total = z_ref[...].astype(F32) + mm_tn(pick_ref[:, :tokens], back_ref[...])
    for ref in more_refs:
        total += ref[...].astype(F32)
    out_ref[...] = total.astype(BF16)


def layer_output(z, pick, back, more):
    tokens, rows = z.shape[0], pick.shape[0]
    return call(
        output_kernel,
        jax.ShapeDtypeStruct((tokens, D), BF16),
        (D // HEADS,),
        [columns(tokens), whole(pick.shape), columns(rows)] + [columns(tokens)] * len(more),
        columns(tokens),
        flops=2 * tokens * D * rows,
        moved=2 * D * rows,
    )(z, pick, back, *more)


def down_kernel(dy_ref, down_ref, out_ref):
    out_ref[...] = mm_nt(dy_ref[...], down_ref[...])


def expert_down_back(dy_rows, down_mat):
    rows, hidden = dy_rows.shape[0], down_mat.shape[0]
    tile = 256
    return call(
        down_kernel,
        jax.ShapeDtypeStruct((rows, hidden), F32),
        (hidden // tile,),
        [
            pl.BlockSpec((rows, D), lambda i: (0, 0)),
            pl.BlockSpec((tile, D), lambda i: (i, 0)),
        ],
        columns(rows, tile),
        flops=2 * rows * hidden * D,
        moved=2 * (rows + hidden) * D,
    )(dy_rows, down_mat)


def expert_kernel(
    me_ref, z_ref, mask_ref, router_ref, gate_ref, up_ref, dh_ref,
    hid_ref, dgp_ref, dup_ref, weight_ref, pair_ref, dg_ref,
):
    experts = router_ref.shape[1]

    @pl.when(pl.program_id(0) == 0)
    def _():
        sig = jax.nn.sigmoid(mm(z_ref[...], router_ref[...]))
        sig *= mask_ref[:, :experts].astype(F32)
        total = jnp.sum(sig, axis=1, keepdims=True)
        lane = lax.broadcasted_iota(jnp.int32, sig.shape, 1)
        mine = jnp.sum(jnp.where(lane == me_ref[0, 0], sig, 0.0), axis=1, keepdims=True)
        some = total > 0
        weight_ref[...] = jnp.where(some, mine / jnp.where(some, total, 1.0), 0.0)
        dg_ref[...] = jnp.zeros_like(dg_ref)

    z = z_ref[...]
    gp = mm(z, gate_ref[...])
    up = mm(z, up_ref[...])
    gs = jax.nn.sigmoid(gp)
    hid = (gp * gs * up).astype(BF16)
    plain = dh_ref[...]
    dg_ref[...] += jnp.sum(plain * hid.astype(F32), axis=1, keepdims=True)
    dh = plain * weight_ref[...]
    hid_ref[...] = hid
    dgp_ref[...] = (dh * up * gs * (1.0 + gp * (1.0 - gs))).astype(BF16)
    dup_ref[...] = (dh * gp * gs).astype(BF16)

    @pl.when(pl.program_id(0) == pl.num_programs(0) - 1)
    def _():
        lane = lax.broadcasted_iota(jnp.int32, pair_ref.shape, 1)
        dg = dg_ref[...]
        high = dg.astype(BF16).astype(F32)
        pair = jnp.where(lane == me_ref[0, 0], high, 0.0)
        pair = jnp.where(lane == me_ref[0, 0] + experts, dg - high, pair)
        pair_ref[...] = pair.astype(BF16)


def expert_forward(me, z_rows, dy_rows, router, gate_mat, up_mat, dh_plain):
    rows, hidden, experts = z_rows.shape[0], gate_mat.shape[1], router.shape[1]
    tile, wide = 256, lanes_of(experts)
    beside = D // wide
    inner = jax.ShapeDtypeStruct((rows, hidden), BF16)
    column = jax.ShapeDtypeStruct((rows, 1), F32)
    pair = jax.ShapeDtypeStruct((rows, lanes_of(2 * experts)), BF16)
    return call(
        expert_kernel,
        (inner, inner, inner, column, pair),
        (hidden // tile,),
        [
            smem(),
            whole((rows, D)),
            pl.BlockSpec((rows, wide), lambda i: (0, beside)),
            whole(router.shape),
            columns(D, tile),
            columns(D, tile),
            columns(rows, tile),
        ],
        (columns(rows, tile),) * 3 + (whole((rows, 1)), whole(pair.shape)),
        scratch=[pltpu.VMEM((rows, 1), F32)],
        flops=4 * rows * hidden * D,
        moved=2 * (rows + 2 * hidden) * D,
    )(me, z_rows, dy_rows, router, gate_mat, up_mat, dh_plain)


def back_kernel(dgp_ref, dup_ref, gate_ref, up_ref, weight_ref, out_ref):
    total = mm_nt(dgp_ref[...], gate_ref[...]) + mm_nt(dup_ref[...], up_ref[...])
    out_ref[...] = (total * weight_ref[...]).astype(BF16)


def expert_back(dgp, dup, gate_mat, up_mat, weight):
    rows, hidden = dgp.shape
    stripe = pl.BlockSpec((WIDTH, hidden), lambda i: (i, 0))
    return call(
        back_kernel,
        jax.ShapeDtypeStruct((rows, D), BF16),
        (D // WIDTH,),
        [whole(dgp.shape), whole(dup.shape), stripe, stripe, whole((rows, 1))],
        columns(rows, WIDTH),
        flops=4 * rows * hidden * D,
        moved=2 * (rows + 2 * hidden) * D,
    )(dgp, dup, gate_mat, up_mat, weight)


def product_kernel(hid_ref, down_ref, weight_ref, out_ref):
    out_ref[...] = (mm(hid_ref[...], down_ref[...]) * weight_ref[...]).astype(BF16)


def expert_product(hid, down_mat, weight):
    rows, hidden = hid.shape
    return call(
        product_kernel,
        jax.ShapeDtypeStruct((rows, D), BF16),
        (D // WIDTH,),
        [whole(hid.shape), columns(hidden, WIDTH), whole((rows, 1))],
        columns(rows, WIDTH),
        flops=2 * rows * hidden * D,
        moved=2 * (rows + hidden) * D,
    )(hid, down_mat, weight)


def weights_kernel(
    z_ref, dy_ref, hid_ref, dgp_ref, dup_ref, weight_ref, gate_ref, up_ref, down_ref
):
    z = z_ref[...]
    gate_ref[...] = mm_tn(z, dgp_ref[...]).astype(BF16)
    up_ref[...] = mm_tn(z, dup_ref[...]).astype(BF16)
    de = (dy_ref[...].astype(F32) * weight_ref[...]).astype(BF16)
    down_ref[...] = mm_tn(hid_ref[...], de).astype(BF16)


def expert_weights(z_rows, dy_rows, hid, dgp, dup, weight):
    rows, hidden = hid.shape
    stripe = pl.BlockSpec((WIDTH, hidden), lambda i: (i, 0))
    return call(
        weights_kernel,
        (
            jax.ShapeDtypeStruct((D, hidden), BF16),
            jax.ShapeDtypeStruct((D, hidden), BF16),
            jax.ShapeDtypeStruct((hidden, D), BF16),
        ),
        (D // WIDTH,),
        [columns(rows, WIDTH), columns(rows, WIDTH)] + [whole(hid.shape)] * 3 + [whole((rows, 1))],
        (stripe, stripe, columns(hidden, WIDTH)),
        flops=6 * rows * hidden * D,
        moved=2 * (2 * rows + 3 * hidden) * D,
    )(z_rows, dy_rows, hid, dgp, dup, weight)


def exchange(rows):
    group = lax.axis_size("ctx")
    shaped = rows.reshape(group, rows.shape[0] // group, rows.shape[1])
    moved = lax.all_to_all(shaped, "ctx", split_axis=0, concat_axis=0, tiled=True)
    return moved.reshape(rows.shape)


def after(value, *earlier):
    return lax.optimization_barrier((value, *earlier))[0]


def swap(block, axis, by=1):
    return lax.ppermute(block, axis, [(i, i ^ by) for i in range(lax.axis_size(axis))])


def peers():
    return [(b % 2, b // 2) for b in range(2 * lax.axis_size("near"))]


def replicate(block, *gate):
    far = swap(block, "far")
    near = range(1, lax.axis_size("near"))
    own = [swap(block, "near", n) for n in near]
    gated = after(far, *gate) if gate else far
    other = [swap(gated, "near", n) for n in near]
    return [block, far] + [x for pair in zip(own, other) for x in pair]


def collect_far(parts):
    far = parts[0]
    near = range(1, lax.axis_size("near"))
    if len(near):
        arrived = [swap(parts[2 * n], "near", n) for n in near]
        far = sum((a.astype(F32) for a in arrived), far.astype(F32)).astype(BF16)
    return far


def collect(parts, far):
    near = range(1, lax.axis_size("near"))
    return [swap(far, "far")] + [swap(parts[2 * n - 1], "near", n) for n in near]


def collect_small(parts):
    near = lax.axis_size("near")
    steps = peers()[1:]
    return [swap(part, ("far", "near"), f * near + n) for part, (f, n) in zip(parts, steps)]


def doublings():
    steps = []
    for axis in ("far", "near"):
        by = 1
        while by < lax.axis_size(axis):
            steps.append((axis, by))
            by *= 2
    return steps


def sum_over(term, steps, gate):
    for axis, by in steps:
        term = term + after(swap(term, axis, by), gate)
    return term


def local(
    queries,
    keys,
    values,
    prior_state,
    norm_gain,
    router_weight,
    expert_ids,
    w_gate,
    w_up,
    w_down,
    cotangent,
):
    q, k, v, dy = queries[0], keys[0], values[0], cotangent[0]
    tokens = q.shape[0]
    experts = router_weight.shape[1]
    cap = max(2, 3 * tokens * TOPK // (2 * experts))
    gate_mat, up_mat, down_mat = w_gate[0], w_up[0], w_down[0]
    prior = prior_state[0]
    gain = norm_gain.reshape(1, D)
    me = jnp.stack([lax.axis_index(ALL), jnp.int32(experts)]).reshape(1, 2).astype(jnp.int32)
    plane = lax.axis_index(("far", "near")).reshape(1, 1).astype(jnp.int32)
    rows = experts * cap

    n = lax.axis_size("ctx")
    ids = expert_ids[0]
    beside = jnp.pad(ids.astype(BF16), ((0, 0), (0, 128 - TOPK)))
    terms = state_terms(k, v).reshape(n, H // n * DH, DH)
    here = to_heads(terms)
    sums = running_sum(here, False)
    dy_blocks = replicate(jnp.concatenate([dy, beside], axis=1), sums)
    earlier = to_heads(sums).reshape(H, DH, DH)
    z, att, sig = attention_forward(q, k, v, prior, earlier, gain, router_weight, ids)
    z_blocks = replicate(z)
    pick, chosen, dy_send = route_gather(plane, after(dy_blocks, z), experts, rows, cap)
    dy_rows = exchange(dy_send)
    z_rows = exchange(gather(pick, chosen, z_blocks, False))

    dh_plain = expert_down_back(dy_rows, down_mat)
    hid, dgp, dup, weight, dg_send = expert_forward(
        me, z_rows, dy_rows, router_weight, gate_mat, up_mat, dh_plain
    )
    dg_back = exchange(dg_send)
    dz_send = expert_back(dgp, dup, gate_mat, up_mat, weight)
    dz_back = exchange(dz_send)
    dg_more = collect_small(partials(pick, after(dg_back, dz_send), tokens))
    dlog, rterm = router_gradient(z, dg_back, dg_more, pick, sig)
    eo_send = expert_product(after(hid, dlog), down_mat, weight)
    steps = doublings()
    rterm = sum_over(rterm, steps[:1], eo_send)
    grad_gate, grad_up, grad_down = expert_weights(
        after(z_rows, rterm), dy_rows, hid, dgp, dup, weight
    )
    rterm = sum_over(rterm, steps[1:], grad_gate)

    dz_parts = partials(pick, after(dz_back, rterm), tokens)
    dz_far = collect_far(dz_parts)
    dz_more = collect(dz_parts, dz_far)
    eo_back = exchange(after(eo_send, *dz_parts))
    datt, dterms = attention_middle(
        q, att, dy, dz_back, dz_more, pick, dlog, gain, router_weight, rterm, n
    )
    there = to_heads(dterms)
    eo_parts = partials(pick, after(eo_back, datt), tokens)
    eo_more = collect(eo_parts, collect_far(eo_parts))
    gq, gk, gv = attention_early(q, k, v, after(datt, *eo_parts), prior, earlier)
    later = to_heads(running_sum(there, True))
    grad_k, grad_v, grad_router = attention_late(k, v, later, gk, gv, experts)
    grad_router = grad_router.T
    output = layer_output(z, pick, eo_back, eo_more)
    return (
        output[None],
        gq[None],
        grad_k[None],
        grad_v[None],
        grad_gate[None],
        grad_up[None],
        grad_down[None],
        grad_router,
    )


def solution(mesh):
    tokens = P(("far", "near"), "ctx", None)
    weights = P(ALL, None, None)
    split = Mesh(
        mesh.devices.reshape(2, mesh.shape["dp"] // 2, mesh.shape["ctx"]), ("far", "near", "ctx")
    )
    placed = (
        tokens,
        tokens,
        tokens,
        P(("far", "near"), None, None, None),
        P(),
        P(),
        tokens,
        weights,
        weights,
        weights,
        tokens,
    )
    return jax.shard_map(
        local,
        mesh=split,
        in_specs=placed,
        out_specs=(tokens, tokens, tokens, tokens, weights, weights, weights, P()),
        check_vma=False,
    )
```

```python
import functools

import jax
import jax.numpy as jnp
from jax import lax
from jax.experimental import pallas as pl
from jax.experimental.pallas import tpu as pltpu
from jax.sharding import Mesh
from jax.sharding import PartitionSpec as P

H = 16
DH = 128
D = 2048
TOPK = 4
HB = 8
WIDTH = 512
HEADS = HB * DH
EPS = 1e-05
ALL = ("far", "near", "ctx")
F32 = jnp.float32
BF16 = jnp.bfloat16
LIMIT = 62 << 20


def mm(a, b):
    return jnp.dot(a, b, preferred_element_type=F32)


def mm_tn(a, b):
    return lax.dot_general(a, b, (((0,), (0,)), ((), ())), preferred_element_type=F32)


def mm_nt(a, b):
    return lax.dot_general(a, b, (((1,), (1,)), ((), ())), preferred_element_type=F32)


def halves(x):
    high = x.astype(BF16)
    return high, (x - high.astype(F32)).astype(BF16)


def thirds(x):
    high, rest = x.astype(BF16), None
    rest = x - high.astype(F32)
    middle = rest.astype(BF16)
    return high, middle, (rest - middle.astype(F32)).astype(BF16)


def causal_mask(n):
    return lax.broadcasted_iota(jnp.int32, (n, n), 0) >= lax.broadcasted_iota(jnp.int32, (n, n), 1)


def head(h):
    return slice(h * DH, (h + 1) * DH)


def call(kernel, out_shape, grid, in_specs, out_specs, scratch=(), flops=0, moved=0):
    return pl.pallas_call(
        kernel,
        out_shape=out_shape,
        grid=grid,
        in_specs=in_specs,
        out_specs=out_specs,
        scratch_shapes=scratch,
        compiler_params=pltpu.CompilerParams(vmem_limit_bytes=LIMIT),
        cost_estimate=pl.CostEstimate(flops=flops, bytes_accessed=moved, transcendentals=0),
    )


def whole(shape):
    return pl.BlockSpec(shape, lambda *_: (0,) * len(shape))


def columns(rows, width=HEADS):
    return pl.BlockSpec((rows, width), lambda i: (0, i))


def per_head(n=HB):
    return pl.BlockSpec((n, DH, DH), lambda i: (i, 0, 0))


def lanes_of(n):
    return -(-n // 128) * 128


def route_kernel(cap, top, plane_ref, *refs):
    *ids_refs, pick_ref, chosen_ref = refs
    tokens = ids_refs[0].shape[0]
    experts = chosen_ref.shape[1]
    rows = pick_ref.shape[0]
    slots = len(ids_refs) * cap
    group = rows // slots
    row = lax.broadcasted_iota(jnp.int32, (rows, experts), 0)
    first = lax.broadcasted_iota(jnp.int32, (rows, experts), 1) - plane_ref[0, 0] * group
    first = first * slots
    owns = (row >= first) & (row < first + slots)
    wanted = jnp.sum(jnp.where(owns, row - first + 1, 0), axis=1, keepdims=True).astype(F32)
    owns = owns.astype(F32).astype(BF16)
    lane = lax.broadcasted_iota(jnp.int32, (tokens, experts), 1)
    earlier = causal_mask(tokens).astype(F32).astype(BF16)
    for b, ref in enumerate(ids_refs):
        ids = ref[...].astype(F32)
        chosen = jnp.zeros((tokens, experts), F32)
        for j in range(top):
            chosen += (ids[:, j : j + 1] == lane.astype(F32)).astype(F32)
        place = chosen * (mm(earlier, chosen.astype(BF16)) + float(b * cap))
        found = mm_nt(owns, place.astype(BF16))
        at = slice(b * tokens, (b + 1) * tokens)
        pick_ref[:, at] = (found == wanted).astype(F32).astype(BF16)
        chosen_ref[at] = chosen


def smem():
    return pl.BlockSpec(memory_space=pltpu.SMEM)


def gather_kernel(masked, pick_ref, chosen_ref, *refs):
    *block_refs, send_ref, stack_ref = refs
    tokens = block_refs[0].shape[0]
    pick = pick_ref[...]
    for b, ref in enumerate(block_refs):
        stack_ref[b * tokens : (b + 1) * tokens] = ref[:, :D]
    for c in range(D // WIDTH):
        at = slice(c * WIDTH, (c + 1) * WIDTH)
        send_ref[:, at] = mm(pick, stack_ref[:, at]).astype(BF16)
    if masked:
        experts = chosen_ref.shape[1]
        if send_ref.shape[1] > D + experts:
            send_ref[:, D:] = jnp.zeros((send_ref.shape[0], send_ref.shape[1] - D), BF16)
        mask = mm(pick, chosen_ref[...].astype(BF16))
        send_ref[:, D : D + experts] = mask.astype(BF16)


def gather(pick, chosen, blocks, masked):
    rows = pick.shape[0]
    width = D + (lanes_of(chosen.shape[1]) if masked else 0)
    return call(
        functools.partial(gather_kernel, masked),
        jax.ShapeDtypeStruct((rows, width), BF16),
        (1,),
        [whole(pick.shape), whole(chosen.shape)] + [whole(blocks[0].shape)] * len(blocks),
        whole((rows, width)),
        scratch=[pltpu.VMEM((pick.shape[1], D), BF16)],
        flops=2 * rows * pick.shape[1] * D,
        moved=2 * rows * D,
    )(pick, chosen, *blocks)


def route_gather_kernel(cap, top, plane_ref, *refs):
    *block_refs, pick_ref, chosen_ref, send_ref, stack_ref = refs
    ids_refs = [ref.at[:, D : D + 128] for ref in block_refs]
    route_kernel(cap, top, plane_ref, *ids_refs, pick_ref, chosen_ref)
    gather_kernel(True, pick_ref, chosen_ref, *block_refs, send_ref, stack_ref)


def route_gather(plane, blocks, experts, rows, cap):
    tokens, n = blocks[0].shape[0], len(blocks)
    width = D + lanes_of(experts)
    return call(
        functools.partial(route_gather_kernel, cap, TOPK),
        (
            jax.ShapeDtypeStruct((rows, n * tokens), BF16),
            jax.ShapeDtypeStruct((n * tokens, experts), F32),
            jax.ShapeDtypeStruct((rows, width), BF16),
        ),
        (1,),
        [smem()] + [whole(blocks[0].shape)] * n,
        (whole((rows, n * tokens)), whole((n * tokens, experts)), whole((rows, width))),
        scratch=[pltpu.VMEM((n * tokens, D), BF16)],
        flops=2 * n * rows * tokens * D,
        moved=2 * rows * D,
    )(plane, *blocks)


def partial_kernel(pick_ref, back_ref, *out_refs):
    tokens, width = out_refs[0].shape
    for b, ref in enumerate(out_refs):
        pick = pick_ref[:, (b + 1) * tokens : (b + 2) * tokens]
        for c in range(0, width, WIDTH):
            at = slice(c, min(c + WIDTH, width))
            ref[:, at] = mm_tn(pick, back_ref[:, at]).astype(BF16)


def partials(pick, back, tokens):
    others = pick.shape[1] // tokens - 1
    rows, width = back.shape
    return call(
        partial_kernel,
        (jax.ShapeDtypeStruct((tokens, width), BF16),) * others,
        (1,),
        [whole(pick.shape), whole(back.shape)],
        (whole((tokens, width)),) * others,
        flops=2 * others * rows * width * tokens,
        moved=2 * rows * width,
    )(pick, back)


def state_kernel(k_ref, v_ref, out_ref):
    for h in range(HB):
        out_ref[h] = mm_tn(k_ref[:, head(h)], v_ref[:, head(h)]).astype(BF16)


def state_terms(k, v):
    tokens = k.shape[0]
    return call(
        state_kernel,
        jax.ShapeDtypeStruct((H, DH, DH), BF16),
        (H // HB,),
        [columns(tokens), columns(tokens)],
        per_head(),
        flops=2 * tokens * D * DH,
        moved=6 * tokens * D,
    )(k, v)


def running_kernel(backwards, states, in_ref, out_ref):
    n, rows, _ = in_ref.shape
    total = jnp.zeros((states, DH), F32)
    for i in reversed(range(n)) if backwards else range(n):
        out_ref[i, :states] = total.astype(BF16)
        total += in_ref[i, :states].astype(F32)
    if rows > states:
        half = (rows - states) // 2
        whole_sum = jnp.zeros((half, DH), F32)
        for i in range(n):
            whole_sum += in_ref[i, states : states + half].astype(F32)
            whole_sum += in_ref[i, states + half :].astype(F32)
        high, low = halves(whole_sum)
        for i in range(n):
            out_ref[i, states : states + half] = high
            out_ref[i, states + half :] = low


def to_heads(block):
    return lax.all_to_all(block, "ctx", split_axis=0, concat_axis=0, tiled=True)


def running_sum(here, backwards):
    states = H // here.shape[0] * DH
    return call(
        functools.partial(running_kernel, backwards, states),
        jax.ShapeDtypeStruct(here.shape, BF16),
        (1,),
        [whole(here.shape)],
        whole(here.shape),
        flops=here.size,
        moved=4 * here.size,
    )(here)


def forward_kernel(
    q_ref, k_ref, v_ref, prior_ref, earlier_ref, gain_ref, router_ref, ids_ref,
    z_ref, att_ref, sig_ref, logits_ref,
):
    tokens = q_ref.shape[0]
    causal = causal_mask(tokens)
    step = pl.program_id(0)

    @pl.when(step == 0)
    def _():
        logits_ref[...] = jnp.zeros_like(logits_ref)

    for h in range(HB):
        q, k, v = q_ref[:, head(h)], k_ref[:, head(h)], v_ref[:, head(h)]
        high, low = halves(prior_ref[h] + earlier_ref[h].astype(F32))
        scores = jnp.where(causal, mm_nt(q, k), 0.0).astype(BF16)
        att = mm(scores, v) + mm(q, high) + mm(q, low)
        mean = jnp.mean(att * att, axis=1, keepdims=True)
        z = (att / jnp.sqrt(mean + EPS) * gain_ref[:, head(h)]).astype(BF16)
        att_ref[:, head(h)] = att
        z_ref[:, head(h)] = z
    logits_ref[...] += mm(z_ref[...], router_ref[...])

    @pl.when(step == pl.num_programs(0) - 1)
    def _():
        experts = sig_ref.shape[1]
        lane = lax.broadcasted_iota(jnp.int32, (tokens, experts), 1)
        chosen = jnp.zeros((tokens, experts), F32)
        for j in range(ids_ref.shape[1]):
            chosen += (ids_ref[:, j : j + 1] == lane).astype(F32)
        sig_ref[...] = jax.nn.sigmoid(logits_ref[...]) * chosen


def attention_forward(q, k, v, prior, earlier, gain, router, ids):
    tokens, experts = q.shape[0], router.shape[1]
    return call(
        forward_kernel,
        (
            jax.ShapeDtypeStruct((tokens, D), BF16),
            jax.ShapeDtypeStruct((tokens, D), F32),
            jax.ShapeDtypeStruct((tokens, experts), F32),
        ),
        (H // HB,),
        [
            columns(tokens),
            columns(tokens),
            columns(tokens),
            per_head(),
            per_head(),
            columns(1),
            pl.BlockSpec((HEADS, experts), lambda i: (i, 0)),
            whole(ids.shape),
        ],
        (columns(tokens), columns(tokens), whole((tokens, experts))),
        scratch=[pltpu.VMEM((tokens, experts), F32)],
        flops=2 * tokens * D * 4 * DH,
        moved=2 * D * 8 * tokens,
    )(q, k, v, prior, earlier, gain, router, ids)


def router_kernel(*refs):
    z_ref, dg_ref, pick_ref, sig_ref, *more_refs, dlog_ref, term_ref = refs
    tokens, experts = sig_ref.shape

    @pl.when(pl.program_id(0) == 0)
    def _():
        sig = sig_ref[...]
        both = mm_tn(pick_ref[:, :tokens], dg_ref[...])
        for ref in more_refs:
            both += ref[...].astype(F32)
        dg = both[:, :experts] + both[:, experts : 2 * experts]
        total = jnp.sum(sig, axis=1, keepdims=True)
        mean = jnp.sum(sig * dg, axis=1, keepdims=True) / total
        dlog = sig * (1.0 - sig) * (dg - mean) / total
        for i, part in enumerate(thirds(dlog)):
            dlog_ref[i] = part

    z = z_ref[...]
    term_ref[...] = mm_tn(dlog_ref[0], z) + mm_tn(dlog_ref[1], z) + mm_tn(dlog_ref[2], z)


def router_gradient(z, back, more, pick, sig):
    tokens, experts = sig.shape
    rows = pick.shape[0]
    wide = lanes_of(2 * experts)
    return call(
        router_kernel,
        (
            jax.ShapeDtypeStruct((3, tokens, experts), BF16),
            jax.ShapeDtypeStruct((experts, D), F32),
        ),
        (D // WIDTH,),
        [
            columns(tokens, WIDTH),
            whole((rows, wide)),
            whole(pick.shape),
            whole(sig.shape),
        ]
        + [whole((tokens, wide))] * len(more),
        (whole((3, tokens, experts)), columns(experts, WIDTH)),
        flops=6 * tokens * experts * D,
        moved=2 * tokens * D,
    )(z, back, pick, sig, *more)


def middle_kernel(*refs):
    q_ref, att_ref, dy_ref, back_ref, pick_ref, dlog_ref, gain_ref, router_ref, rterm_ref = refs[:9]
    *more_refs, datt_ref, term_ref = refs[9:]
    experts = router_ref.shape[1]
    per = HB // term_ref.shape[0]
    tokens = q_ref.shape[0]
    router = router_ref[...]
    dz = dy_ref[...].astype(F32) + mm_tn(pick_ref[:, :tokens], back_ref[...])
    for ref in more_refs:
        dz += ref[...].astype(F32)
    for i in range(3):
        dz += mm_nt(dlog_ref[i], router)
    weighted = dz * gain_ref[...]
    for h in range(HB):
        att, w = att_ref[:, head(h)], weighted[:, head(h)]
        mean = jnp.mean(att * att, axis=1, keepdims=True) + EPS
        inner = jnp.sum(w * att, axis=1, keepdims=True)
        datt = ((w - att * (inner / (DH * mean))) / jnp.sqrt(mean)).astype(BF16)
        datt_ref[:, head(h)] = datt
        to, i = h // per, h % per
        term_ref[to, head(i)] = mm_tn(q_ref[:, head(h)], datt).astype(BF16)
        high, low = halves(rterm_ref[:, head(h)])
        at = per * DH + i * experts
        term_ref[to, at : at + experts] = high
        term_ref[to, at + per * experts : at + per * experts + experts] = low


def attention_middle(q, att, dy, back, more, pick, dlog, gain, router, rterm, n):
    tokens, rows, experts = q.shape[0], pick.shape[0], router.shape[1]
    per = H // n
    length = per * (DH + 2 * experts)
    return call(
        middle_kernel,
        (
            jax.ShapeDtypeStruct((tokens, D), BF16),
            jax.ShapeDtypeStruct((n, length, DH), BF16),
        ),
        (H // HB,),
        [
            columns(tokens),
            columns(tokens),
            columns(tokens),
            columns(rows),
            whole(pick.shape),
            whole(dlog.shape),
            columns(1),
            pl.BlockSpec((HEADS, experts), lambda i: (i, 0)),
            columns(experts),
        ]
        + [columns(tokens)] * len(more),
        (columns(tokens), pl.BlockSpec((HB // per, length, DH), lambda i: (i, 0, 0))),
        flops=2 * tokens * D * (DH + rows + 3 * experts),
        moved=2 * D * (8 * tokens + rows),
    )(q, att, dy, back, pick, dlog, gain, router, rterm, *more)


def early_kernel(q_ref, k_ref, v_ref, datt_ref, prior_ref, earlier_ref, gq_ref, gk_ref, gv_ref):
    causal = causal_mask(q_ref.shape[0])
    for h in range(HB):
        q, k, v = q_ref[:, head(h)], k_ref[:, head(h)], v_ref[:, head(h)]
        datt = datt_ref[:, head(h)]
        high, low = halves(prior_ref[h] + earlier_ref[h].astype(F32))
        dscores = jnp.where(causal, mm_nt(datt, v), 0.0).astype(BF16)
        scores = jnp.where(causal, mm_nt(q, k), 0.0).astype(BF16)
        gq = mm(dscores, k) + mm_nt(datt, high) + mm_nt(datt, low)
        gq_ref[:, head(h)] = gq.astype(BF16)
        gk_ref[:, head(h)] = mm_tn(dscores, q)
        gv_ref[:, head(h)] = mm_tn(scores, datt)


def attention_early(q, k, v, datt, prior, earlier):
    tokens = q.shape[0]
    block = columns(tokens)
    return call(
        early_kernel,
        (
            jax.ShapeDtypeStruct((tokens, D), BF16),
            jax.ShapeDtypeStruct((tokens, D), F32),
            jax.ShapeDtypeStruct((tokens, D), F32),
        ),
        (H // HB,),
        [block, block, block, block, per_head(), per_head()],
        (block, block, block),
        flops=2 * tokens * D * DH * 7,
        moved=22 * D * tokens,
    )(q, k, v, datt, prior, earlier)


def late_kernel(k_ref, v_ref, later_ref, gk_ref, gv_ref, out_k_ref, out_v_ref, router_ref):
    experts = router_ref.shape[0]
    per = HB // later_ref.shape[0]
    for h in range(HB):
        to, i = h // per, h % per
        later = later_ref[to, head(i)]
        out_k_ref[:, head(h)] = (gk_ref[:, head(h)] + mm_nt(v_ref[:, head(h)], later)).astype(BF16)
        out_v_ref[:, head(h)] = (gv_ref[:, head(h)] + mm(k_ref[:, head(h)], later)).astype(BF16)
        at = per * DH + i * experts
        high = later_ref[to, at : at + experts].astype(F32)
        low = later_ref[to, at + per * experts : at + per * experts + experts].astype(F32)
        router_ref[:, head(h)] = high + low


def attention_late(k, v, later, gk, gv, experts):
    tokens = k.shape[0]
    block = columns(tokens)
    out = jax.ShapeDtypeStruct((tokens, D), BF16)
    n, length, _ = later.shape
    return call(
        late_kernel,
        (out, out, jax.ShapeDtypeStruct((experts, D), F32)),
        (H // HB,),
        [
            block,
            block,
            pl.BlockSpec((HB * n // H, length, DH), lambda i: (i, 0, 0)),
            block,
            block,
        ],
        (block, block, columns(experts)),
        flops=2 * tokens * D * DH * 2,
        moved=18 * D * tokens,
    )(k, v, later, gk, gv)


def output_kernel(z_ref, pick_ref, back_ref, *refs):
    *more_refs, out_ref = refs
    tokens = z_ref.shape[0]
    total = z_ref[...].astype(F32) + mm_tn(pick_ref[:, :tokens], back_ref[...])
    for ref in more_refs:
        total += ref[...].astype(F32)
    out_ref[...] = total


def layer_output(z, pick, back, more):
    tokens, rows = z.shape[0], pick.shape[0]
    return call(
        output_kernel,
        jax.ShapeDtypeStruct((tokens, D), F32),
        (D // HEADS,),
        [columns(tokens), whole(pick.shape), columns(rows)] + [columns(tokens)] * len(more),
        columns(tokens),
        flops=2 * tokens * D * rows,
        moved=2 * D * rows,
    )(z, pick, back, *more)


def down_kernel(dy_ref, down_ref, out_ref):
    out_ref[...] = mm_nt(dy_ref[...], down_ref[...])


def expert_down_back(dy_rows, down_mat):
    rows, hidden = dy_rows.shape[0], down_mat.shape[0]
    tile = 256
    return call(
        down_kernel,
        jax.ShapeDtypeStruct((rows, hidden), F32),
        (hidden // tile,),
        [
            pl.BlockSpec((rows, D), lambda i: (0, 0)),
            pl.BlockSpec((tile, D), lambda i: (i, 0)),
        ],
        columns(rows, tile),
        flops=2 * rows * hidden * D,
        moved=2 * (rows + hidden) * D,
    )(dy_rows, down_mat)


def expert_kernel(
    me_ref, z_ref, mask_ref, router_ref, gate_ref, up_ref, dh_ref,
    hid_ref, dgp_ref, dup_ref, weight_ref, pair_ref, dg_ref,
):
    experts = router_ref.shape[1]

    @pl.when(pl.program_id(0) == 0)
    def _():
        sig = jax.nn.sigmoid(mm(z_ref[...], router_ref[...]))
        sig *= mask_ref[:, :experts].astype(F32)
        total = jnp.sum(sig, axis=1, keepdims=True)
        lane = lax.broadcasted_iota(jnp.int32, sig.shape, 1)
        mine = jnp.sum(jnp.where(lane == me_ref[0, 0], sig, 0.0), axis=1, keepdims=True)
        some = total > 0
        weight_ref[...] = jnp.where(some, mine / jnp.where(some, total, 1.0), 0.0)
        dg_ref[...] = jnp.zeros_like(dg_ref)

    z = z_ref[...]
    gp = mm(z, gate_ref[...])
    up = mm(z, up_ref[...])
    gs = jax.nn.sigmoid(gp)
    hid = (gp * gs * up).astype(BF16)
    plain = dh_ref[...]
    dg_ref[...] += jnp.sum(plain * hid.astype(F32), axis=1, keepdims=True)
    dh = plain * weight_ref[...]
    hid_ref[...] = hid
    dgp_ref[...] = (dh * up * gs * (1.0 + gp * (1.0 - gs))).astype(BF16)
    dup_ref[...] = (dh * gp * gs).astype(BF16)

    @pl.when(pl.program_id(0) == pl.num_programs(0) - 1)
    def _():
        lane = lax.broadcasted_iota(jnp.int32, pair_ref.shape, 1)
        dg = dg_ref[...]
        high = dg.astype(BF16).astype(F32)
        pair = jnp.where(lane == me_ref[0, 0], high, 0.0)
        pair = jnp.where(lane == me_ref[0, 0] + experts, dg - high, pair)
        pair_ref[...] = pair.astype(BF16)


def expert_forward(me, z_rows, dy_rows, router, gate_mat, up_mat, dh_plain):
    rows, hidden, experts = z_rows.shape[0], gate_mat.shape[1], router.shape[1]
    tile, wide = 256, lanes_of(experts)
    beside = D // wide
    inner = jax.ShapeDtypeStruct((rows, hidden), BF16)
    column = jax.ShapeDtypeStruct((rows, 1), F32)
    pair = jax.ShapeDtypeStruct((rows, lanes_of(2 * experts)), BF16)
    return call(
        expert_kernel,
        (inner, inner, inner, column, pair),
        (hidden // tile,),
        [
            smem(),
            whole((rows, D)),
            pl.BlockSpec((rows, wide), lambda i: (0, beside)),
            whole(router.shape),
            columns(D, tile),
            columns(D, tile),
            columns(rows, tile),
        ],
        (columns(rows, tile),) * 3 + (whole((rows, 1)), whole(pair.shape)),
        scratch=[pltpu.VMEM((rows, 1), F32)],
        flops=4 * rows * hidden * D,
        moved=2 * (rows + 2 * hidden) * D,
    )(me, z_rows, dy_rows, router, gate_mat, up_mat, dh_plain)


def back_kernel(dgp_ref, dup_ref, gate_ref, up_ref, weight_ref, out_ref):
    total = mm_nt(dgp_ref[...], gate_ref[...]) + mm_nt(dup_ref[...], up_ref[...])
    out_ref[...] = (total * weight_ref[...]).astype(BF16)


def expert_back(dgp, dup, gate_mat, up_mat, weight):
    rows, hidden = dgp.shape
    stripe = pl.BlockSpec((WIDTH, hidden), lambda i: (i, 0))
    return call(
        back_kernel,
        jax.ShapeDtypeStruct((rows, D), BF16),
        (D // WIDTH,),
        [whole(dgp.shape), whole(dup.shape), stripe, stripe, whole((rows, 1))],
        columns(rows, WIDTH),
        flops=4 * rows * hidden * D,
        moved=2 * (rows + 2 * hidden) * D,
    )(dgp, dup, gate_mat, up_mat, weight)


def product_kernel(hid_ref, down_ref, weight_ref, out_ref):
    out_ref[...] = (mm(hid_ref[...], down_ref[...]) * weight_ref[...]).astype(BF16)


def expert_product(hid, down_mat, weight):
    rows, hidden = hid.shape
    return call(
        product_kernel,
        jax.ShapeDtypeStruct((rows, D), BF16),
        (D // WIDTH,),
        [whole(hid.shape), columns(hidden, WIDTH), whole((rows, 1))],
        columns(rows, WIDTH),
        flops=2 * rows * hidden * D,
        moved=2 * (rows + hidden) * D,
    )(hid, down_mat, weight)


def weights_kernel(
    z_ref, dy_ref, hid_ref, dgp_ref, dup_ref, weight_ref, gate_ref, up_ref, down_ref
):
    z = z_ref[...]
    gate_ref[...] = mm_tn(z, dgp_ref[...]).astype(BF16)
    up_ref[...] = mm_tn(z, dup_ref[...]).astype(BF16)
    de = (dy_ref[...].astype(F32) * weight_ref[...]).astype(BF16)
    down_ref[...] = mm_tn(hid_ref[...], de).astype(BF16)


def expert_weights(z_rows, dy_rows, hid, dgp, dup, weight):
    rows, hidden = hid.shape
    stripe = pl.BlockSpec((WIDTH, hidden), lambda i: (i, 0))
    return call(
        weights_kernel,
        (
            jax.ShapeDtypeStruct((D, hidden), BF16),
            jax.ShapeDtypeStruct((D, hidden), BF16),
            jax.ShapeDtypeStruct((hidden, D), BF16),
        ),
        (D // WIDTH,),
        [columns(rows, WIDTH), columns(rows, WIDTH)] + [whole(hid.shape)] * 3 + [whole((rows, 1))],
        (stripe, stripe, columns(hidden, WIDTH)),
        flops=6 * rows * hidden * D,
        moved=2 * (2 * rows + 3 * hidden) * D,
    )(z_rows, dy_rows, hid, dgp, dup, weight)


def exchange(rows):
    group = lax.axis_size("ctx")
    shaped = rows.reshape(group, rows.shape[0] // group, rows.shape[1])
    moved = lax.all_to_all(shaped, "ctx", split_axis=0, concat_axis=0, tiled=True)
    return moved.reshape(rows.shape)


def after(value, *earlier):
    return lax.optimization_barrier((value, *earlier))[0]


def swap(block, axis, by=1):
    return lax.ppermute(block, axis, [(i, i ^ by) for i in range(lax.axis_size(axis))])


def peers():
    return [(b % 2, b // 2) for b in range(2 * lax.axis_size("near"))]


def replicate(block, *gate):
    far = swap(block, "far")
    near = range(1, lax.axis_size("near"))
    own = [swap(block, "near", n) for n in near]
    gated = after(far, *gate) if gate else far
    other = [swap(gated, "near", n) for n in near]
    return [block, far] + [x for pair in zip(own, other) for x in pair]


def collect_far(parts):
    far = parts[0]
    near = range(1, lax.axis_size("near"))
    if len(near):
        arrived = [swap(parts[2 * n], "near", n) for n in near]
        far = sum((a.astype(F32) for a in arrived), far.astype(F32)).astype(BF16)
    return far


def collect(parts, far):
    near = range(1, lax.axis_size("near"))
    return [swap(far, "far")] + [swap(parts[2 * n - 1], "near", n) for n in near]


def collect_small(parts):
    near = lax.axis_size("near")
    steps = peers()[1:]
    return [swap(part, ("far", "near"), f * near + n) for part, (f, n) in zip(parts, steps)]


def doublings():
    steps = []
    for axis in ("far", "near"):
        by = 1
        while by < lax.axis_size(axis):
            steps.append((axis, by))
            by *= 2
    return steps


def sum_over(term, steps, gate):
    for axis, by in steps:
        term = term + after(swap(term, axis, by), gate)
    return term


def local(
    queries,
    keys,
    values,
    prior_state,
    norm_gain,
    router_weight,
    expert_ids,
    w_gate,
    w_up,
    w_down,
    cotangent,
):
    q, k, v, dy = queries[0], keys[0], values[0], cotangent[0]
    tokens = q.shape[0]
    experts = router_weight.shape[1]
    cap = max(2, 3 * tokens * TOPK // (2 * experts))
    gate_mat, up_mat, down_mat = w_gate[0], w_up[0], w_down[0]
    prior = prior_state[0]
    gain = norm_gain.reshape(1, D)
    me = jnp.stack([lax.axis_index(ALL), jnp.int32(experts)]).reshape(1, 2).astype(jnp.int32)
    plane = lax.axis_index(("far", "near")).reshape(1, 1).astype(jnp.int32)
    rows = experts * cap

    n = lax.axis_size("ctx")
    ids = expert_ids[0]
    beside = jnp.pad(ids.astype(BF16), ((0, 0), (0, 128 - TOPK)))
    terms = state_terms(k, v).reshape(n, H // n * DH, DH)
    here = to_heads(terms)
    sums = running_sum(here, False)
    dy_blocks = replicate(jnp.concatenate([dy, beside], axis=1), sums)
    earlier = to_heads(sums).reshape(H, DH, DH)
    z, att, sig = attention_forward(q, k, v, prior, earlier, gain, router_weight, ids)
    z_blocks = replicate(z)
    pick, chosen, dy_send = route_gather(plane, after(dy_blocks, z), experts, rows, cap)
    dy_rows = exchange(dy_send)
    z_rows = exchange(gather(pick, chosen, z_blocks, False))

    dh_plain = expert_down_back(dy_rows, down_mat)
    hid, dgp, dup, weight, dg_send = expert_forward(
        me, z_rows, dy_rows, router_weight, gate_mat, up_mat, dh_plain
    )
    dg_back = exchange(dg_send)
    dz_send = expert_back(dgp, dup, gate_mat, up_mat, weight)
    dz_back = exchange(dz_send)
    dg_more = collect_small(partials(pick, after(dg_back, dz_send), tokens))
    dlog, rterm = router_gradient(z, dg_back, dg_more, pick, sig)
    eo_send = expert_product(after(hid, dlog), down_mat, weight)
    steps = doublings()
    rterm = sum_over(rterm, steps[:1], eo_send)
    grad_gate, grad_up, grad_down = expert_weights(
        after(z_rows, rterm), dy_rows, hid, dgp, dup, weight
    )
    rterm = sum_over(rterm, steps[1:], grad_gate)

    dz_parts = partials(pick, after(dz_back, rterm), tokens)
    dz_far = collect_far(dz_parts)
    dz_more = collect(dz_parts, dz_far)
    eo_back = exchange(after(eo_send, *dz_parts))
    datt, dterms = attention_middle(
        q, att, dy, dz_back, dz_more, pick, dlog, gain, router_weight, rterm, n
    )
    there = to_heads(dterms)
    eo_parts = partials(pick, after(eo_back, datt), tokens)
    eo_more = collect(eo_parts, collect_far(eo_parts))
    gq, gk, gv = attention_early(q, k, v, after(datt, *eo_parts), prior, earlier)
    later = to_heads(running_sum(there, True))
    grad_k, grad_v, grad_router = attention_late(k, v, later, gk, gv, experts)
    grad_router = grad_router.T
    own = layer_output(z, pick, after(eo_back, gq), [])
    output = sum((x.astype(F32) for x in eo_more), own).astype(BF16)
    return (
        output[None],
        gq[None],
        grad_k[None],
        grad_v[None],
        grad_gate[None],
        grad_up[None],
        grad_down[None],
        grad_router,
    )


def solution(mesh):
    tokens = P(("far", "near"), "ctx", None)
    weights = P(ALL, None, None)
    split = Mesh(
        mesh.devices.reshape(2, mesh.shape["dp"] // 2, mesh.shape["ctx"]), ("far", "near", "ctx")
    )
    placed = (
        tokens,
        tokens,
        tokens,
        P(("far", "near"), None, None, None),
        P(),
        P(),
        tokens,
        weights,
        weights,
        weights,
        tokens,
    )
    return jax.shard_map(
        local,
        mesh=split,
        in_specs=placed,
        out_specs=(tokens, tokens, tokens, tokens, weights, weights, weights, P()),
        check_vma=False,
    )
```
